128 devices in a mesh: tm: 32 (over x, z, core), space: 4 (over y).
Axes of the slice: x: 4, y: 4, z: 4, core: 2. Of those that a mesh axis runs over, the one named last changes fastest.
Arguments:
- observations: bfloat16 [8192, 32, 4, 512], P(None, 'tm', 'space'), may hold values from -6 to 6
- pod_basis: bfloat16 [32, 4, 512, 1024], P(None, 'space'), may hold values from -0.0234375 to 0.0234375
- decay: float32 [8192, 1024], P('tm', 'space'), may hold values from 0 to 1
- step_mask: int32 [8192], P('tm'), may hold values 0 or 1
- process_var: float32 [1024], P('space'), may hold values from 0.00012207031 to 1
- obs_var: float32 [1024], P('space'), may hold values from 1 to 512
- prior_mean: float32 [1024], P('space'), may hold values from -6 to 6
- prior_var: float32 [1024], P('space'), may hold values from 0.5 to 4
Outputs:
- coefficients: float32 [8192, 1024], P('tm', 'space')
- filtered_mean: float32 [8192, 1024], P('tm', 'space')
- smoothed_mean: float32 [8192, 1024], P('tm', 'space')
- log_variance: float32 [8192, 1024], P('tm', 'space')
The draws below stay inside these ranges and needn't reach their ends.
All inputs are finite; a program needn't handle non-finite values. No bound on the sum of `step_mask` on one device may be relied on, other than what follows from the above.
Results may differ from the reference program's by a relative error of at most 0.0003.
Values may be sent and summed in bfloat16 or wider, within the bound.
A program may use at most 256 MiB of HBM per device.

```python
import math
import jax
import jax.numpy as jnp
from jax import lax

K = 1024
CB = 512
STEPS = 8192
GRID_T = 32
GRID_S = 4
CELLS = 65536


def draw_decay(key, part):
    key_rate, key_rough, key_place, key_loss = jax.random.split(key, 4)
    low_rate = math.log(0.5 / STEPS)
    high_rate = math.log(1.0 / 30.0)
    rates = jnp.exp(jax.random.uniform(key_rate, (K,), jnp.float32, low_rate, high_rate))
    rough = jnp.exp(jax.random.uniform(key_rough, (STEPS, K), jnp.float32, math.log(0.5), math.log(2.0)))
    places = jax.random.randint(key_place, (3,), 0, STEPS)
    struck = jnp.any(jnp.arange(STEPS)[:, None] == places[None, :], axis=1)
    losses = jax.random.uniform(key_loss, (STEPS, K), jnp.float32, 0.5, 0.8)
    factors = jnp.exp(-rates[None, :] * rough) * jnp.where(struck[:, None], losses, 1.0)
    return factors.astype(jnp.float32)


def touch_ends(drawn, stream_key, smallest, high):
    dims = drawn.shape
    place = [jax.random.randint(jax.random.fold_in(stream_key, axis), (), 0, dims[axis]) for axis in range(len(dims))]
    drawn = drawn.at[tuple(place)].set(smallest)
    longest = dims.index(max(dims))
    place[longest] = (place[longest] + 1) % dims[longest]
    return drawn.at[tuple(place)].set(high)


def spiked(entries, rng, source, target, parts, factor):
    def block_of(position):
        return (jnp.arange(entries.shape[position]) // (entries.shape[position] // parts)).reshape((-1,) + (1,) * (entries.ndim - 1 - position))

    near = jax.random.permutation(rng, parts)[block_of(target)]
    second = (block_of(target) + parts // 2) % parts
    return jnp.where((block_of(source) == near) | (block_of(source) == second), factor * entries, entries)


def block_levels(key, shape, cuts, low, top_value):
    gain, own = 1.0, jax.random.fold_in(key, 6)
    for dim, parts in cuts:
        steps = jnp.exp(jax.random.uniform(jax.random.fold_in(own, dim), (parts,), jnp.float32, low / len(cuts), top_value / len(cuts)))
        gain = gain * jnp.repeat(steps, shape[dim] // parts).reshape([-1 if axis == dim else 1 for axis in range(len(shape))])
    return gain


def bell_draw(stream_key, shape, deviation, limit, cuts=(), kind=jnp.bfloat16):
    array = deviation * jax.random.normal(stream_key, shape, jnp.float32)
    if cuts:
        array = array * block_levels(stream_key, shape, cuts, -0.22, 0.18)
    return jnp.clip(array, -limit, limit).astype(kind)


def gaussian_with(own_key, extent, spread, most, cuts, heavy, dtype=jnp.bfloat16):
    array = spread * jax.random.normal(own_key, extent, jnp.float32)
    if cuts:
        array = array * block_levels(own_key, extent, cuts, -0.22, 0.18)
    return jnp.clip(spiked(array, jax.random.fold_in(own_key, 3), *heavy), -most, most).astype(dtype)


def setup_inputs(seed: int = 0) -> dict:
    seeds = jax.random.split(jax.random.key(seed), 9)
    return {
        "observations": gaussian_with(seeds[0], (STEPS, GRID_T, GRID_S, CB), 1.0, 6.0, ((1, 32), (2, 4)), (1, 0, 32, 2.75)),
        "pod_basis": bell_draw(seeds[1], (GRID_T, GRID_S, CB, K), CELLS ** -0.5, 0.0234375, ((1, 4),)),
        "decay": draw_decay(jax.random.fold_in(seeds[8], 71), 0),
        "step_mask": touch_ends((jax.random.randint(seeds[3], (STEPS,), 0, 2) < 1).astype(jnp.int32), jax.random.fold_in(seeds[3], 1), 0, 1),
        "process_var": jnp.clip(jnp.exp(math.log(1.0) - 9.010913 * jax.random.uniform(seeds[4], (K,), jnp.float32) ** block_levels(seeds[4], (K,), ((0, 4),), -0.2, 0.2)), 0.00012207031, 1.0),
        "obs_var": jnp.clip(jnp.exp(math.log(512.0) - 6.2383246 * jax.random.uniform(seeds[5], (K,), jnp.float32) ** block_levels(seeds[5], (K,), ((0, 4),), -0.2, 0.2)), 1.0, 512.0),
        "prior_mean": bell_draw(seeds[6], (K,), 1.0, 6.0, ((0, 4),), jnp.float32),
        "prior_var": jnp.clip(jnp.exp(math.log(4.0) - 2.0794415 * jax.random.uniform(seeds[7], (K,), jnp.float32) ** block_levels(seeds[7], (K,), ((0, 4),), -0.2, 0.2)), 0.5, 4.0),
    }


def reference(observations, pod_basis, decay, step_mask, process_var, obs_var, prior_mean, prior_var):
    flat_obs = observations.reshape(observations.shape[0], -1)
    flat_pod = pod_basis.reshape(-1, pod_basis.shape[-1])
    coefficients = jnp.dot(flat_obs, flat_pod, preferred_element_type=jnp.float32)
    observed = step_mask.astype(jnp.float32)

    def update(pred_mean, pred_var, target, flag):
        denominator = pred_var + obs_var
        kalman_gain = flag * pred_var / denominator
        retain = (obs_var + (1.0 - flag) * pred_var) / denominator
        return pred_mean + kalman_gain * (target - pred_mean), retain * pred_var

    start_mean, start_var = update(prior_mean, prior_var, coefficients[0], observed[0])

    def forward(carry, inputs):
        last_mean, last_var = carry
        factor, target, flag = inputs
        new_mean, new_var = update(factor * last_mean, factor * factor * last_var + process_var, target, flag)
        return (new_mean, new_var), (new_mean, new_var)

    _, (means, variances) = lax.scan(forward, (start_mean, start_var), (decay[1:], coefficients[1:], observed[1:]))
    filtered_mean = jnp.concatenate([start_mean[None], means], 0)
    filtered_var = jnp.concatenate([start_var[None], variances], 0)

    def backward(carry, inputs):
        later_mean, later_var = carry
        here_mean, here_var, factor = inputs
        predicted = factor * factor * here_var + process_var
        smoother_gain = here_var * factor / predicted
        new_mean = here_mean + smoother_gain * (later_mean - factor * here_mean)
        new_var = smoother_gain * smoother_gain * later_var + here_var * process_var / predicted
        return (new_mean, new_var), (new_mean, new_var)

    _, (smooth_means, smooth_vars) = lax.scan(backward, (filtered_mean[-1], filtered_var[-1]), (filtered_mean[:-1], filtered_var[:-1], decay[1:]), reverse=True)
    smoothed_mean = jnp.concatenate([smooth_means, filtered_mean[-1:]], 0)
    smoothed_var = jnp.concatenate([smooth_vars, filtered_var[-1:]], 0)
    return coefficients, filtered_mean, smoothed_mean, jnp.log(smoothed_var)
```

```python
import jax
import jax.numpy as jnp
from jax import lax
from jax.experimental import pallas as pl
from jax.experimental.pallas import tpu as pltpu
from jax.sharding import PartitionSpec as P

MESH = pl.DeviceIdType.MESH
F32 = jnp.float32
BF16 = jnp.bfloat16
I16 = jnp.int16

UNIT = (96, 80, 80)
START = (0, 96, 176)
ORDER = (("x", "y", "z"), ("y", "z", "x"), ("z", "x", "y"))
ROWS = tuple(64 * u for u in UNIT)
LIMIT = 32760.0
TINY = 1e-33

MESSAGES = ((2, 0, 1), (2, 1, -1), (1, 0, 1), (1, 1, 1), (3, 0, -1), (3, 1, -1))


def stage_rows(part, stage):
    return ROWS[part] // 4 ** (stage + 1)


def half_rows(part, stage, half):
    rows = stage_rows(part, stage)
    first = rows // 2 if stage < 2 else 48
    return (0, first) if half == 0 else (first, rows - first)


def chunk_rows(part, rows):
    return UNIT[part] if rows % UNIT[part] == 0 else rows


def kernel(obs, basis, decay, mask, q_ref, r_ref, pm_ref, pv_ref, coef_out, fm_out, sm_out, lv_out, *scratch):
    (fa, fb, fc, qa, qb, qc, ra1, ra2, ra3, rb1, rb2, rb3, rc1, rc2, rc3, oa, ob, oc, bas, scale_out, scale_in,
     dec, flag, qv, vv, aa, kk, gg, ww, ap, sm, gs, sv, cc, ll, s0, small, e1, e2, e3, g1, g2, g3, mi,
     own_sem, part_sem, psend_sem, bas_sem, send_sem, recv_sem, ssend_sem, srecv_sem, esend_sem, erecv_sem) = scratch
    acc = (fa, fb, fc)
    quant = (qa, qb, qc)
    landed = ((ra1, ra2, ra3), (rb1, rb2, rb3), (rc1, rc2, rc3))
    tm = lax.axis_index("tm")
    y = lax.axis_index("space")
    x, z, core = tm // 8, lax.rem(tm // 2, 4), lax.rem(tm, 2)
    partner = tm + 1 - 2 * core

    def turn(value, by, count):
        return lax.rem(value + by, count)

    def neighbour(axis, way):
        if axis == "x":
            return {"tm": turn(tm, 8 if way > 0 else 24, 32)}
        if axis == "z":
            return {"tm": x * 8 + turn(z, 1 if way > 0 else 3, 4) * 2 + core}
        return {"space": turn(y, 1 if way > 0 else 3, 4)}

    barrier = pltpu.get_barrier_semaphore()

    def greet(step, carry):
        pl.semaphore_signal(barrier, inc=1, device_id={"tm": turn(tm, step, 32)}, device_id_type=MESH)
        return carry

    lax.fori_loop(1, 32, greet, 0)
    for way in (1, -1):
        pl.semaphore_signal(barrier, inc=1, device_id=neighbour("y", way), device_id_type=MESH)

    def obs_copies(part, slot):
        rows = slice(START[part], START[part] + UNIT[part])
        pieces = []
        for other in range(4):
            if part == 0:
                at, to = (turn(x, slot, 4), turn(z, other, 4)), oa.at[slot, other]
            elif part == 1:
                at, to = (turn(x, other, 4), turn(z, slot, 4)), ob.at[slot, other]
            else:
                at, to = (turn(x, other, 4), turn(z, slot, 4)), oc.at[slot, other]
            pieces.append((at, rows, to))
        return pieces

    tasks = [(0, 2), (1, 0), (1, 1), (1, 2), (1, 3), (2, 2), (0, 1), (0, 3), (2, 1), (2, 3), (0, 0), (2, 0)]
    held = (oa, ob, oc)
    for yr in range(4):
        columns = pl.ds(pl.multiple_of(turn(y, yr, 4) * 256, 256), 256)
        for side, who in ((0, tm), (1, partner)):
            pltpu.make_async_copy(
                basis.at[who, :, columns], bas.at[yr, pl.ds(side * 512, 512)], bas_sem.at[yr]
            ).start()
    for part, slot in tasks:
        for (xi, zi), rows, to in obs_copies(part, slot):
            pltpu.make_async_copy(obs.at[xi, zi, core, rows], to.at[:, 0:512], own_sem.at[part, slot]).start()

    dec[0, 0:256, :] = decay[:, 0:128]
    dec[1, 0:256, :] = decay[:, 128:256]
    first = tm == 0
    for h in range(2):
        lanes = slice(h * 128, h * 128 + 128)
        e1[3:4, lanes] = dec[h, 0:1, :]
        qv[h] = jnp.broadcast_to(q_ref[:, lanes], (256, 128))
        qv[h, 0:1, :] = jnp.where(first, pv_ref[:, lanes], q_ref[:, lanes])
        dec[h, 0:1, :] = jnp.where(first, 0.0, dec[h, 0:1, :])
    row = lax.broadcasted_iota(jnp.int32, (256, 256), 0)
    column = lax.broadcasted_iota(jnp.int32, (256, 256), 1)
    spread_mask = jnp.where(row == column, jnp.broadcast_to(mask[...].astype(F32), (256, 256)), 0.0).astype(BF16)
    flag[...] = jnp.dot(spread_mask, jnp.ones((256, 128), BF16), preferred_element_type=F32)

    noise = [jnp.broadcast_to(r_ref[:, h * 128 : h * 128 + 128], (8, 128)) for h in range(2)]
    process = [jnp.broadcast_to(q_ref[:, h * 128 : h * 128 + 128], (8, 128)) for h in range(2)]

    def steps(s):
        return pl.ds(s, 8, stride=32)

    def join(early, late):
        lead_e, spread_e, weight_e = early
        lead_l, spread_l, weight_l = late
        factor = 1.0 / (1.0 + spread_e * weight_l)
        return (
            lead_l * factor * lead_e,
            lead_l * lead_l * factor * spread_e + spread_l,
            lead_e * lead_e * factor * weight_l + weight_e,
        )

    def compose(s, carry):
        seen = flag[steps(s), :]
        out = []
        for h in range(2):
            d, q = dec[h, steps(s), :], qv[h, steps(s), :]
            den = 1.0 / (q + noise[h])
            retain = (noise[h] + (1.0 - seen) * q) * den
            out.append(join(carry[h], (retain * d, retain * q, seen * d * d * den)))
        return tuple(out)

    one, nil = jnp.ones((8, 128), F32), jnp.zeros((8, 128), F32)
    chunks = lax.fori_loop(0, 32, compose, ((one, nil, nil), (one, nil, nil)))
    for h in range(2):
        lanes = slice(h * 128, h * 128 + 128)
        total = tuple(part[0:1] for part in chunks[h])
        for k in range(1, 8):
            total = join(total, tuple(part[k : k + 1] for part in chunks[h]))
        for i in range(3):
            e1[i : i + 1, lanes] = total[i]
            small[i, h] = chunks[h][i]

    pl.semaphore_wait(barrier, 33)

    for part, slot in tasks:
        for (xi, zi), rows, to in obs_copies(part, slot):
            pltpu.make_async_remote_copy(
                obs.at[xi, zi, 1 - core, rows],
                to.at[:, 512:1024],
                psend_sem.at[part, slot],
                part_sem.at[part, slot],
                device_id={"tm": partner},
                device_id_type=MESH,
            ).start()

    def scatter(number, mine, gathered):
        gathered[tm] = mine[...]

        def push(step, carry):
            pltpu.make_async_remote_copy(
                mine,
                gathered.at[tm],
                esend_sem.at[number],
                erecv_sem.at[number],
                device_id={"tm": turn(tm, step, 32)},
                device_id_type=MESH,
            ).start()
            return carry

        lax.fori_loop(1, 32, push, 0)

    def gathered_wait(number, gathered):
        some = gathered.at[pl.ds(0, 31)]
        pltpu.make_async_copy(some, some, erecv_sem.at[number]).wait()

    def scattered_wait(number, gathered):
        some = gathered.at[pl.ds(0, 31)]
        pltpu.make_async_copy(some, some, esend_sem.at[number]).wait()

    scatter(0, e1, g1)

    def obs_wait(part, slot):
        to = held[part].at[slot, :, :, pl.ds(0, 512)]
        pltpu.make_async_copy(to, to, own_sem.at[part, slot]).wait()
        pltpu.make_async_copy(to, to, part_sem.at[part, slot]).wait()

    def project(part, slot):
        u = UNIT[part]

        def block(k, carry):
            if part == 0:
                left, right, to = oa[slot], bas[k], (slot * 4 + k) * 384
            elif part == 1:
                left, right, to = ob[k], bas[slot], (slot * 4 + k) * 320
            else:
                left, right, to = oc[slot], bas[k], slot * 1280 + k * 80
            total = jnp.dot(left.reshape(4 * u, 1024), right, preferred_element_type=F32)
            if part < 2:
                acc[part][pl.ds(pl.multiple_of(to, 16), 4 * u), :] = total
            else:
                for xr in range(4):
                    acc[part][pl.ds(pl.multiple_of(to + xr * 320, 16), 80), :] = total[xr * 80 : xr * 80 + 80]
            return carry

        lax.fori_loop(0, 4, block, 0)

    def place(part, stage, message):
        slot, half, _ = MESSAGES[message]
        begin, rows = half_rows(part, stage, half)
        return slot * stage_rows(part, stage) + begin, rows

    def peak(block):
        return jnp.max(jnp.abs(block).reshape(-1, 8, 256), axis=0)

    def copies(part, stage, message):
        _, _, way = MESSAGES[message]
        begin, rows = place(part, stage, message)
        to = neighbour(ORDER[part][stage], way)
        number = (part * 3 + stage) * 6 + message
        return (
            pltpu.make_async_remote_copy(
                quant[part].at[pl.ds(begin, rows)],
                landed[part][stage].at[message, pl.ds(0, rows)],
                send_sem.at[number],
                recv_sem.at[number],
                device_id=to,
                device_id_type=MESH,
            ),
            pltpu.make_async_remote_copy(
                scale_out.at[number],
                scale_in.at[number],
                ssend_sem.at[number],
                srecv_sem.at[number],
                device_id=to,
                device_id_type=MESH,
            ),
        )

    def recv_wait(part, stage, message):
        for copy in copies(part, stage, message):
            copy.wait_recv()

    def send(part, stage, message, relayed=None):
        begin, rows = place(part, stage, message)
        number = (part * 3 + stage) * 6 + message
        size = chunk_rows(part, rows)
        if relayed is not None:
            recv_wait(part, stage, relayed)
            factor = scale_in[(part * 3 + stage) * 6 + relayed]

        def measure(k, top):
            at = pl.ds(pl.multiple_of(begin + k * size, 16), size)
            block = acc[part][at, :]
            if relayed is not None:
                came = landed[part][stage][relayed, pl.ds(pl.multiple_of(k * size, 16), size), :]
                block = block + came.astype(F32) * factor
                acc[part][at, :] = block
            return jnp.maximum(top, peak(block))

        top = lax.fori_loop(0, rows // size, measure, jnp.zeros((8, 256), F32))
        top = jnp.maximum(jnp.max(top, axis=0, keepdims=True), TINY)
        scale_out[number] = top * (1.0 / LIMIT)
        inverse = LIMIT / top

        def encode(k, carry):
            at = pl.ds(pl.multiple_of(begin + k * size, 16), size)
            quant[part][at, :] = jnp.round(acc[part][at, :] * inverse).astype(I16)
            return carry

        lax.fori_loop(0, rows // size, encode, 0)
        for copy in copies(part, stage, message):
            copy.start()

    def finish(part, stage):
        for half, (left, right) in enumerate(((2, 4), (3, 5))):
            begin, rows = half_rows(part, stage, half)
            size = chunk_rows(part, rows)
            for message in (left, right):
                recv_wait(part, stage, message)
            scales = [scale_in[(part * 3 + stage) * 6 + m] for m in (left, right)]

            def add(k, carry):
                at = pl.ds(pl.multiple_of(begin + k * size, 16), size)
                block = acc[part][at, :]
                for m, factor in zip((left, right), scales):
                    came = landed[part][stage][m, pl.ds(pl.multiple_of(k * size, 16), size), :]
                    block = block + came.astype(F32) * factor
                acc[part][at, :] = block
                return carry

            lax.fori_loop(0, rows // size, add, 0)

    for yr in range(4):
        pltpu.make_async_copy(bas.at[yr], bas.at[yr], bas_sem.at[yr]).wait()
    for part in range(3):
        if part == 1:
            for slot in range(4):
                obs_wait(1, slot)
        else:
            obs_wait(part, 2)
        project(part, 2)
        send(part, 0, 0)
        send(part, 0, 1)
    for slot, message in ((1, 3), (3, 4)):
        for part in range(3):
            if part != 1:
                obs_wait(part, slot)
            project(part, slot)
            send(part, 0, message)

    gathered_wait(0, g1)

    def enter(k, v):
        new = []
        for h in range(2):
            lanes = slice(h * 128, h * 128 + 128)
            lead, spread, weight = (g1[k, i : i + 1, lanes] for i in range(3))
            new.append(jnp.where(k < tm, lead * lead * v[h] / (1.0 + weight * v[h]) + spread, v[h]))
        return tuple(new)

    v = lax.fori_loop(0, 31, enter, (jnp.zeros((1, 128), F32),) * 2)
    after = turn(tm, 1, 32)
    for h in range(2):
        lanes = slice(h * 128, h * 128 + 128)
        dec[h, 256:257, :] = jnp.where(tm == 31, 0.0, g1[after, 3:4, lanes])
        now = v[h]
        for k in range(8):
            small[3, h, k : k + 1, :] = now
            lead, spread, weight = (small[i, h, k : k + 1, :] for i in range(3))
            now = lead * lead * now / (1.0 + weight * now) + spread

    def forward(s, carry):
        seen = flag[steps(s), :]
        out = []
        for h in range(2):
            v, prefix = carry[h]
            d, q = dec[h, steps(s), :], qv[h, steps(s), :]
            vp = d * d * v + q
            den = 1.0 / (vp + noise[h])
            retain = (noise[h] + (1.0 - seen) * vp) * den
            v = retain * vp
            a = retain * d
            prefix = prefix * a
            vv[h, steps(s), :] = v
            aa[h, steps(s), :] = a
            kk[h, steps(s), :] = seen * vp * den
            ap[h, steps(s), :] = prefix
            out.append((v, prefix))
        return tuple(out)

    ends = lax.fori_loop(0, 32, forward, tuple((small[3, h], one) for h in range(2)))

    def backward(i, carry):
        s = 31 - i
        out = []
        for h in range(2):
            var, pull, suffix = carry[h]
            nd, v = dec[h, steps(s + 1), :], vv[h, steps(s), :]
            inverse = 1.0 / (nd * nd * v + process[h])
            g, w = v * nd * inverse, process[h] * inverse
            var = g * g * var + v * w
            pull = g * pull + w * ap[h, steps(s), :]
            suffix = g * suffix
            gg[h, steps(s), :] = g
            ww[h, steps(s), :] = w
            sv[h, steps(s), :] = var
            sm[h, steps(s), :] = pull
            gs[h, steps(s), :] = suffix
            out.append((var, pull, suffix))
        return tuple(out)

    heads = lax.fori_loop(0, 32, backward, ((nil, nil, one), (nil, nil, one)))
    for h in range(2):
        lanes = slice(h * 128, h * 128 + 128)
        var, pull, suffix = heads[h]
        last = ends[h][1]
        small[4, h], small[5, h], small[6, h] = last, pull, suffix
        small[7, h] = var
        m = jnp.ones((1, 128), F32)
        starts = []
        for k in range(8):
            starts.append(m)
            m = m * last[k : k + 1]
        e2[0:1, lanes] = m
        s_var, s_pull, s_suffix = jnp.zeros((1, 128), F32), jnp.zeros((1, 128), F32), jnp.ones((1, 128), F32)
        for k in range(7, -1, -1):
            g = suffix[k : k + 1]
            s_var = var[k : k + 1] + g * g * s_var
            s_pull = pull[k : k + 1] * starts[k] + g * s_pull
            s_suffix = g * s_suffix
        e2[1:2, lanes], e2[2:3, lanes], e2[3:4, lanes] = s_pull, s_suffix, s_var
    scatter(1, e2, g2)

    for part in range(3):
        send(part, 0, 2, relayed=0)
        send(part, 0, 5, relayed=1)
    for part in range(3):
        if part != 1:
            obs_wait(part, 0)
        project(part, 0)

    gathered_wait(1, g2)

    def leave(i, v):
        k = 31 - i
        new = []
        for h in range(2):
            lanes = slice(h * 128, h * 128 + 128)
            suffix, var = g2[k, 2:3, lanes], g2[k, 3:4, lanes]
            new.append(jnp.where(k > tm, var + suffix * suffix * v[h], v[h]))
        return tuple(new)

    v = lax.fori_loop(0, 31, leave, (jnp.zeros((1, 128), F32),) * 2)
    for h in range(2):
        lanes = slice(h * 128, h * 128 + 128)
        now = v[h]
        for k in range(7, -1, -1):
            rows = slice(k * 32, k * 32 + 32)
            g = gs[h, rows, :]
            lv_out[rows, lanes] = jnp.log(sv[h, rows, :] + g * g * now)
            g = small[6, h, k : k + 1, :]
            now = small[7, h, k : k + 1, :] + g * g * now

    for stage in range(3):
        for part in range(3):
            finish(part, stage)
            if stage < 2:
                for message in (0, 1, 3, 4):
                    send(part, stage + 1, message)
        if stage < 2:
            for part in range(3):
                send(part, stage + 1, 2, relayed=0)
                send(part, stage + 1, 5, relayed=1)

    for part in range(3):
        rows = slice(START[part], START[part] + UNIT[part])
        block = acc[part][0 : UNIT[part], :]
        coef_out[rows, :] = block
        for h in range(2):
            cc[h, rows, :] = block[:, h * 128 : h * 128 + 128] * kk[h, rows, :]
    for h in range(2):
        lanes = slice(h * 128, h * 128 + 128)
        pv, r = pv_ref[:, lanes], r_ref[:, lanes]
        retain = (r + (1.0 - flag[0:1, :]) * pv) / (pv + r)
        cc[h, 0:1, :] = cc[h, 0:1, :] + jnp.where(first, retain * pm_ref[:, lanes], 0.0)

    def mean_forward(s, carry):
        out = []
        for h in range(2):
            m = aa[h, steps(s), :] * carry[h] + cc[h, steps(s), :]
            ll[h, steps(s), :] = m
            out.append(m)
        return tuple(out)

    tails = lax.fori_loop(0, 32, mean_forward, (nil, nil))

    def mean_backward(i, carry):
        s = 31 - i
        out = []
        for h in range(2):
            m = gg[h, steps(s), :] * carry[h] + ww[h, steps(s), :] * ll[h, steps(s), :]
            s0[h, steps(s), :] = m
            out.append(m)
        return tuple(out)

    fronts = lax.fori_loop(0, 32, mean_backward, (nil, nil))

    def chain(h, m, s):
        into, back = [], [None] * 8
        for k in range(8):
            into.append(m)
            m = small[4, h, k : k + 1, :] * m + tails[h][k : k + 1]
        for k in range(7, -1, -1):
            back[k] = s
            s = fronts[h][k : k + 1] + small[5, h, k : k + 1, :] * into[k] + small[6, h, k : k + 1, :] * s
        return into, back, m, s

    zero = jnp.zeros((1, 128), F32)
    for h in range(2):
        lanes = slice(h * 128, h * 128 + 128)
        _, _, m, s = chain(h, zero, zero)
        e3[0:1, lanes], e3[1:2, lanes] = m, s
    scatter(2, e3, g3)
    gathered_wait(2, g3)

    def means(k, m):
        mi[k] = m
        return g2[k, 0:1, :] * m + g3[k, 0:1, :]

    lax.fori_loop(0, 32, means, jnp.zeros((1, 256), F32))

    def smooths(i, s):
        k = 31 - i
        new = g3[k, 1:2, :] + g2[k, 1:2, :] * mi[k] + g2[k, 2:3, :] * s
        return jnp.where(k > tm, new, s)

    s_in = lax.fori_loop(0, 31, smooths, jnp.zeros((1, 256), F32))
    m_in = mi[tm]
    for h in range(2):
        lanes = slice(h * 128, h * 128 + 128)
        into, back, _, _ = chain(h, m_in[:, lanes], s_in[:, lanes])
        for k in range(8):
            rows = slice(k * 32, k * 32 + 32)
            fm_out[rows, lanes] = ll[h, rows, :] + ap[h, rows, :] * into[k]
            sm_out[rows, lanes] = s0[h, rows, :] + sm[h, rows, :] * into[k] + gs[h, rows, :] * back[k]

    for part, slot in tasks:
        to = held[part].at[slot, :, :, pl.ds(0, 512)]
        pltpu.make_async_copy(to, to, psend_sem.at[part, slot]).wait()
    for part in range(3):
        for stage in range(3):
            for message in range(6):
                for copy in copies(part, stage, message):
                    copy.wait_send()
    scattered_wait(0, g1)
    scattered_wait(1, g2)
    scattered_wait(2, g3)


def body(observations, pod_basis, decay, step_mask, process_var, obs_var, prior_mean, prior_var):
    block = (256, 256)
    vmem = pl.BlockSpec(memory_space=pltpu.VMEM)
    anywhere = pl.BlockSpec(memory_space=pl.ANY)
    plane = pltpu.VMEM((2, 256, 128), F32)
    landing = [
        pltpu.VMEM((6, half_rows(p, s, 0)[1], 256), I16) for p in range(3) for s in range(3)
    ]
    dma = pltpu.SemaphoreType.DMA
    scratch = [
        *[pltpu.VMEM((rows, 256), F32) for rows in ROWS],
        *[pltpu.VMEM((rows, 256), I16) for rows in ROWS],
        *landing,
        *[pltpu.VMEM((4, 4, u, 1024), BF16) for u in UNIT],
        pltpu.VMEM((4, 1024, 256), BF16),
        pltpu.VMEM((54, 1, 256), F32),
        pltpu.VMEM((54, 1, 256), F32),
        pltpu.VMEM((2, 264 + 24, 128), F32),
        pltpu.VMEM((256, 128), F32),
        *[plane] * 13,
        pltpu.VMEM((8, 2, 8, 128), F32),
        pltpu.VMEM((4, 256), F32),
        pltpu.VMEM((4, 256), F32),
        pltpu.VMEM((2, 256), F32),
        pltpu.VMEM((32, 4, 256), F32),
        pltpu.VMEM((32, 4, 256), F32),
        pltpu.VMEM((32, 2, 256), F32),
        pltpu.VMEM((32, 1, 256), F32),
        dma((3, 4)),
        dma((3, 4)),
        dma((3, 4)),
        dma((4,)),
        dma((54,)),
        dma((54,)),
        dma((54,)),
        dma((54,)),
        dma((3,)),
        dma((3,)),
    ]
    return tuple(
        pl.pallas_call(
            kernel,
            out_shape=[jax.ShapeDtypeStruct(block, F32)] * 4,
            in_specs=[anywhere, anywhere, *[vmem] * 6],
            out_specs=[vmem] * 4,
            scratch_shapes=scratch,
            compiler_params=pltpu.CompilerParams(
                collective_id=0, has_side_effects=True, vmem_limit_bytes=60 * 2**20
            ),
        )(
            observations.reshape(4, 4, 2, 256, 512),
            pod_basis.reshape(32, 512, 1024),
            decay,
            step_mask.reshape(1, 256),
            process_var.reshape(1, 256),
            obs_var.reshape(1, 256),
            prior_mean.reshape(1, 256),
            prior_var.reshape(1, 256),
        )
    )


def solution(mesh):
    return jax.shard_map(
        body,
        mesh=mesh,
        in_specs=(
            P(None, "tm", "space", None),
            P(None, "space", None, None),
            P("tm", "space"),
            P("tm"),
            P("space"),
            P("space"),
            P("space"),
            P("space"),
        ),
        out_specs=(P("tm", "space"), P("tm", "space"), P("tm", "space"), P("tm", "space")),
        check_vma=False,
    )
```

```python
import jax
import jax.numpy as jnp
from jax import lax
from jax.experimental import pallas as pl
from jax.experimental.pallas import tpu as pltpu
from jax.sharding import PartitionSpec as P

MESH = pl.DeviceIdType.MESH
F32 = jnp.float32
BF16 = jnp.bfloat16
I16 = jnp.int16

UNIT = (96, 64, 96)
START = (0, 96, 160)
ORDER = (("x", "y", "z"), ("y", "z", "x"), ("z", "y", "x"))
ROWS = tuple(64 * u for u in UNIT)
LIMIT = 32760.0
TINY = 1e-33
TURNS = (0, 2, 1)

MESSAGES = ((2, 0, 1), (2, 1, -1), (1, 0, 1), (1, 1, 1), (3, 0, -1), (3, 1, -1))


def turn(value, by, count):
    return lax.rem(value + by, count)


def sub_block(i):
    return lax.rem(2 + 3 * i + 3 * (i // 2) + 2 * (i // 3), 4)


def lane(h):
    return slice(h * 128, h * 128 + 128)


def kernel(obs, basis, decay, mask, q_ref, r_ref, pm_ref, pv_ref, *refs):
    outs, scratch = refs[:8], refs[8:]
    (made, last, made_sem, fa, fb, fc, qa, qb, qc, ra1, ra2, ra3, rb1, rb2, rb3, rc1, rc2, rc3, oa, ob, oc, bas, scale_out, scale_in,
     dec, flag, qv, vv, aa, kk, gg, ww, ap, sm, gs, sv, cc, ll, s0, small, e1, e2, e3, g1, g2, g3, wm, ws, wl,
     own_sem, part_sem, psend_sem, bas_sem, send_sem, recv_sem, ssend_sem, srecv_sem, esend_sem, erecv_sem) = scratch
    def put(i):
        source = last if i == 7 else made.at[i]
        return pltpu.make_async_copy(source, outs[i], made_sem.at[i])

    acc = (fa, fb, fc)
    quant = (qa, qb, qc)
    landed = ((ra1, ra2, ra3), (rb1, rb2, rb3), (rc1, rc2, rc3))
    held = (oa, ob, oc)
    tm = lax.axis_index("tm")
    y = lax.axis_index("space")
    x, z, core = tm // 8, lax.rem(tm // 2, 4), lax.rem(tm, 2)
    partner = tm + 1 - 2 * core

    def neighbour(axis, way):
        if axis == "x":
            return {"tm": turn(tm, 8 if way > 0 else 24, 32)}
        if axis == "z":
            return {"tm": x * 8 + turn(z, 1 if way > 0 else 3, 4) * 2 + core}
        return {"space": turn(y, 1 if way > 0 else 3, 4)}

    barrier = pltpu.get_barrier_semaphore()

    def greet(step, carry):
        pl.semaphore_signal(barrier, inc=1, device_id={"tm": turn(tm, step, 32)}, device_id_type=MESH)
        return carry

    lax.fori_loop(1, 32, greet, 0)
    for way in (1, -1):
        pl.semaphore_signal(barrier, inc=1, device_id=neighbour("y", way), device_id_type=MESH)

    def obs_copies(part, slot):
        rows = slice(START[part], START[part] + UNIT[part])
        pieces = []
        for other in range(4):
            at = (turn(x, slot, 4), turn(z, other, 4)) if part == 0 else (turn(x, other, 4), turn(z, slot, 4))
            pieces.append((at, rows, held[part].at[slot, other]))
        return pieces

    tasks = [(0, 2), (2, 2), (1, 2), (1, 1), (1, 3), (1, 0), (0, 1), (0, 3), (0, 0), (2, 1), (2, 3), (2, 0)]
    for yr in (2, 1, 3, 0):
        columns = pl.ds(pl.multiple_of(turn(y, yr, 4) * 256, 256), 256)
        for side, who in ((0, tm), (1, partner)):
            pltpu.make_async_copy(
                basis.at[who, :, columns], bas.at[yr, pl.ds(side * 512, 512)], bas_sem.at[yr]
            ).start()
    for part, slot in tasks:
        for (xi, zi), rows, to in obs_copies(part, slot):
            pltpu.make_async_copy(obs.at[xi, zi, core, rows], to.at[:, 0:512], own_sem.at[part, slot]).start()

    first = tm == 0
    for h in range(2):
        dec[h, 0:256, :] = decay[:, lane(h)]
        e1[3:4, lane(h)] = dec[h, 0:1, :]
        qv[h] = jnp.broadcast_to(q_ref[:, lane(h)], (256, 128))
        qv[h, 0:1, :] = jnp.where(first, pv_ref[:, lane(h)], q_ref[:, lane(h)])
        dec[h, 0:1, :] = jnp.where(first, 0.0, dec[h, 0:1, :])
    row = lax.broadcasted_iota(jnp.int32, (256, 256), 0)
    column = lax.broadcasted_iota(jnp.int32, (256, 256), 1)
    spread_mask = jnp.where(row == column, jnp.broadcast_to(mask[...].astype(F32), (256, 256)), 0.0).astype(BF16)
    flag[...] = jnp.dot(spread_mask, jnp.ones((256, 128), BF16), preferred_element_type=F32)

    def wide(ref, h):
        return jnp.broadcast_to(ref[:, lane(h)], (8, 128))

    blocks = [(g, h) for g in range(2) for h in range(2)]

    def steps(s, g):
        return pl.ds(g * 128 + s, 8, stride=16)

    def join(early, late):
        lead_e, spread_e, weight_e = early
        lead_l, spread_l, weight_l = late
        factor = 1.0 / (1.0 + spread_e * weight_l)
        return (
            lead_l * factor * lead_e,
            lead_l * lead_l * factor * spread_e + spread_l,
            lead_e * lead_e * factor * weight_l + weight_e,
        )

    def compose(s, carry):
        out = []
        for (g, h), early in zip(blocks, carry):
            seen, d, q = flag[steps(s, g), :], dec[h, steps(s, g), :], qv[h, steps(s, g), :]
            noise = wide(r_ref, h)
            den = 1.0 / (q + noise)
            retain = (noise + (1.0 - seen) * q) * den
            out.append(join(early, (retain * d, retain * q, seen * d * d * den)))
        return tuple(out)

    one, nil = jnp.ones((8, 128), F32), jnp.zeros((8, 128), F32)
    unit, zero = jnp.ones((1, 128), F32), jnp.zeros((1, 128), F32)
    chunks = lax.fori_loop(0, 16, compose, ((one, nil, nil),) * 4, unroll=2)
    totals = []
    for (g, h), parts in zip(blocks, chunks):
        for i in range(3):
            small[i, h, g * 8 : g * 8 + 8, :] = parts[i]
        totals.append(tuple(part[0:1] for part in parts))
    for k in range(1, 8):
        totals = [join(t, tuple(p[k : k + 1] for p in parts)) for t, parts in zip(totals, chunks)]
    for h in range(2):
        for i, value in enumerate(join(totals[h], totals[2 + h])):
            e1[i : i + 1, lane(h)] = value
        for i in range(3):
            small[11 + i, h, 0:1, :] = totals[h][i]

    pl.semaphore_wait(barrier, 33)

    for part, slot in tasks:
        for (xi, zi), rows, to in obs_copies(part, slot):
            pltpu.make_async_remote_copy(
                obs.at[xi, zi, 1 - core, rows],
                to.at[:, 512:1024],
                psend_sem.at[part, slot],
                part_sem.at[part, slot],
                device_id={"tm": partner},
                device_id_type=MESH,
            ).start()

    def scatter(number, mine, gathered):
        gathered[tm] = mine[...]

        def push(step, carry):
            pltpu.make_async_remote_copy(
                mine,
                gathered.at[tm],
                esend_sem.at[number],
                erecv_sem.at[number],
                device_id={"tm": turn(tm, step, 32)},
                device_id_type=MESH,
            ).start()
            return carry

        lax.fori_loop(1, 32, push, 0)

    def gathered_wait(number, gathered, sem):
        some = gathered.at[pl.ds(0, 31)]
        pltpu.make_async_copy(some, some, sem.at[number]).wait()

    scatter(0, e1, g1)

    def obs_wait(part, slot):
        to = held[part].at[slot, :, :, pl.ds(0, 512)]
        pltpu.make_async_copy(to, to, own_sem.at[part, slot]).wait()
        pltpu.make_async_copy(to, to, part_sem.at[part, slot]).wait()

    def product(part, slot, j):
        u = UNIT[part]
        obs_slot, mode_slot = (j, slot) if part == 1 else (slot, j)
        return jnp.dot(held[part][obs_slot].reshape(4 * u, 1024), bas[mode_slot], preferred_element_type=F32)

    def place(part, stage, message, j):
        slot, half, _ = MESSAGES[message]
        u = UNIT[part]
        if stage == 0:
            return (slot * 4 + j) * (4 * u) + half * (2 * u), 2 * u
        if stage == 1:
            return slot * 4 * u + half * 2 * u, 2 * u
        return slot * u + half * (u // 2), u // 2

    def number_of(part, stage, message, j):
        return part * 36 + (j * 6 if stage == 0 else 18 + 6 * stage) + message

    def index_of(stage, message, j):
        return j * 6 + message if stage == 0 else message

    def peak(block):
        return jnp.max(jnp.abs(block).reshape(-1, 8, 256), axis=0)

    def steps_of(top):
        top = jnp.maximum(jnp.max(top, axis=0, keepdims=True), TINY)
        return top * (1.0 / LIMIT), LIMIT / top

    def copies(part, stage, message, j):
        begin, rows = place(part, stage, message, j)
        to = neighbour(ORDER[part][stage], MESSAGES[message][2])
        number = number_of(part, stage, message, j)
        return (
            pltpu.make_async_remote_copy(
                quant[part].at[pl.ds(pl.multiple_of(begin, 16), rows)],
                landed[part][stage].at[index_of(stage, message, j)],
                send_sem.at[part, stage],
                recv_sem.at[number],
                device_id=to,
                device_id_type=MESH,
            ),
            pltpu.make_async_remote_copy(
                scale_out.at[number],
                scale_in.at[number],
                ssend_sem.at[part, stage],
                srecv_sem.at[number],
                device_id=to,
                device_id_type=MESH,
            ),
        )

    def recv_wait(part, stage, message, j):
        for copy in copies(part, stage, message, j):
            copy.wait_recv()

    def send(part, stage, message, j=0, relayed=None):
        begin, rows = place(part, stage, message, j)
        number = number_of(part, stage, message, j)
        size = min(rows, 64)
        if relayed is not None:
            recv_wait(part, stage, relayed, j)
            factor = scale_in[number_of(part, stage, relayed, j)]

        def measure(k, top):
            at = pl.ds(pl.multiple_of(begin + k * size, 16), size)
            block = acc[part][at, :]
            if relayed is not None:
                came = landed[part][stage][index_of(stage, relayed, j), pl.ds(pl.multiple_of(k * size, 16), size), :]
                block = block + came.astype(F32) * factor
                acc[part][at, :] = block
            return jnp.maximum(top, peak(block))

        top = lax.fori_loop(0, rows // size, measure, jnp.zeros((8, 256), F32))
        scale_out[number], inverse = steps_of(top)

        def encode(k, carry):
            at = pl.ds(pl.multiple_of(begin + k * size, 16), size)
            quant[part][at, :] = jnp.round(acc[part][at, :] * inverse).astype(I16)
            return carry

        lax.fori_loop(0, rows // size, encode, 0)
        for copy in copies(part, stage, message, j):
            copy.start()

    def far(part, j):
        total = product(part, 2, j)
        u = UNIT[part]
        for message in (0, 1):
            begin, rows = place(part, 0, message, j)
            block = total[message * 2 * u : message * 2 * u + 2 * u]
            scale_out[number_of(part, 0, message, j)], inverse = steps_of(peak(block))
            at = pl.ds(pl.multiple_of(begin, 16), rows)
            quant[part][at, :] = jnp.round(block * inverse).astype(I16)
            for copy in copies(part, 0, message, j):
                copy.start()

    def rest(part, j):
        u = UNIT[part]

        def block(k, carry):
            slot = lax.rem(1 + 2 * k + 3 * (k // 2), 4)
            acc[part][pl.ds(pl.multiple_of((slot * 4 + j) * (4 * u), 16), 4 * u), :] = product(part, slot, j)
            return carry

        lax.fori_loop(0, 3, block, 0)
        send(part, 0, 3, j)
        send(part, 0, 4, j)

    def finish(part, stages, j=0):
        u = UNIT[part]
        rows = u // 2 if stages == (2,) else 2 * u
        size = min(rows, 64)
        for half, pair in enumerate(((2, 4), (3, 5))):
            begin = half * rows + (j * (4 * u) if stages == (0,) else 0)
            came = [(stage, message) for stage in stages for message in pair]
            for stage, message in came:
                recv_wait(part, stage, message, j)
            scales = [scale_in[number_of(part, stage, m, j)] for stage, m in came]

            def add(k, carry):
                at = pl.ds(pl.multiple_of(begin + k * size, 16), size)
                block = acc[part][at, :]
                for (stage, m), factor in zip(came, scales):
                    rows_in = pl.ds(pl.multiple_of(k * size, 16), size)
                    block = block + landed[part][stage][index_of(stage, m, j), rows_in, :].astype(F32) * factor
                acc[part][at, :] = block
                return carry

            lax.fori_loop(0, rows // size, add, 0)

    def variances():
        gathered_wait(0, g1, erecv_sem)

        def enter(k, v):
            lead, spread, weight = (g1[k, i : i + 1, :] for i in range(3))
            return jnp.where(k < tm, lead * lead * v / (1.0 + weight * v) + spread, v)

        v = lax.fori_loop(0, 31, enter, jnp.zeros((1, 256), F32), unroll=2)
        after = turn(tm, 1, 32)
        now = []
        for h in range(2):
            dec[h, 256:257, :] = jnp.where(tm == 31, 0.0, g1[after, 3:4, lane(h)])
            now.append(v[:, lane(h)])
        for h in range(2):
            lead, spread, weight = (small[11 + i, h, 0:1, :] for i in range(3))
            now.append(lead * lead * now[h] / (1.0 + weight * now[h]) + spread)
        for k in range(8):
            for b, (g, h) in enumerate(blocks):
                at = slice(g * 8 + k, g * 8 + k + 1)
                small[3, h, at, :] = now[b]
                if k < 7:
                    lead, spread, weight = (small[i, h, at, :] for i in range(3))
                    now[b] = lead * lead * now[b] / (1.0 + weight * now[b]) + spread

        def forward(s, carry):
            out = []
            for (g, h), (v, prefix) in zip(blocks, carry):
                seen, d, q = flag[steps(s, g), :], dec[h, steps(s, g), :], qv[h, steps(s, g), :]
                noise = wide(r_ref, h)
                vp = d * d * v + q
                den = 1.0 / (vp + noise)
                retain = (noise + (1.0 - seen) * vp) * den
                v = retain * vp
                a = retain * d
                prefix = prefix * a
                vv[h, steps(s, g), :] = v
                aa[h, steps(s, g), :] = a
                kk[h, steps(s, g), :] = seen * vp * den
                ap[h, steps(s, g), :] = prefix
                out.append((v, prefix))
            return tuple(out)

        starts = tuple((small[3, h, g * 8 : g * 8 + 8, :], one) for g, h in blocks)
        ends = lax.fori_loop(0, 16, forward, starts, unroll=2)
        for (g, h), (_, prefix) in zip(blocks, ends):
            small[4, h, g * 8 : g * 8 + 8, :] = prefix

    def smoother():
        def backward(i, carry):
            s = 15 - i
            out = []
            for (g, h), (var, pull, suffix) in zip(blocks, carry):
                nd, v = dec[h, steps(s + 1, g), :], vv[h, steps(s, g), :]
                process = wide(q_ref, h)
                inverse = 1.0 / (nd * nd * v + process)
                gain, w = v * nd * inverse, process * inverse
                var = gain * gain * var + v * w
                pull = gain * pull + w * ap[h, steps(s, g), :]
                suffix = gain * suffix
                gg[h, steps(s, g), :] = gain
                ww[h, steps(s, g), :] = w
                sv[h, steps(s, g), :] = var
                sm[h, steps(s, g), :] = pull
                gs[h, steps(s, g), :] = suffix
                out.append((var, pull, suffix))
            return tuple(out)

        heads = lax.fori_loop(0, 16, backward, ((nil, nil, one),) * 4, unroll=2)
        for (g, h), (var, pull, suffix) in zip(blocks, heads):
            rows = slice(g * 8, g * 8 + 8)
            small[5, h, rows, :], small[6, h, rows, :], small[7, h, rows, :] = pull, suffix, var
        for h in range(2):
            m = unit
            for k in range(16):
                small[8, h, k : k + 1, :] = m
                m = m * small[4, h, k : k + 1, :]
            e2[0:1, lane(h)] = m
            s_var, s_pull, s_suffix = zero, zero, unit
            for k in range(15, -1, -1):
                at = slice(k, k + 1)
                small[9, h, at, :], small[10, h, at, :] = s_pull, s_suffix
                g = small[6, h, at, :]
                s_var = small[7, h, at, :] + g * g * s_var
                s_pull = small[5, h, at, :] * small[8, h, at, :] + g * s_pull
                s_suffix = g * s_suffix
            e2[1:2, lane(h)], e2[2:3, lane(h)], e2[3:4, lane(h)] = s_pull, s_suffix, s_var
        scatter(1, e2, g2)

    def weights():
        gathered_wait(1, g2, erecv_sem)

        def down(i, carry):
            k = 31 - i
            var, w = carry
            prefix, suffix, spread = g2[k, 0:1, :], g2[k, 2:3, :], g2[k, 3:4, :]
            wm[k] = jnp.where(k < tm, w, 0.0)
            return (
                jnp.where(k > tm, spread + suffix * suffix * var, var),
                jnp.where(k < tm, prefix * w, w),
            )

        var, _ = lax.fori_loop(0, 32, down, (jnp.zeros((1, 256), F32), jnp.ones((1, 256), F32)), unroll=2)

        def up(k, w):
            ws[k] = jnp.where(k > tm, w, 0.0)
            return jnp.where(k > tm, g2[k, 2:3, :] * w, w)

        lax.fori_loop(0, 32, up, jnp.ones((1, 256), F32), unroll=2)

        def across(i, pull):
            k = 31 - i
            wl[k] = pull
            return ws[k] * g2[k, 1:2, :] + g2[k, 0:1, :] * pull

        lax.fori_loop(0, 32, across, jnp.zeros((1, 256), F32), unroll=2)
        for h in range(2):
            now = var[:, lane(h)]
            for k in range(15, -1, -1):
                rows, at = slice(k * 16, k * 16 + 16), slice(k, k + 1)
                g = gs[h, rows, :]
                prefix, pull, suffix = (small[i, h, at, :] for i in (8, 9, 10))
                made[6, rows, lane(h)] = jnp.log(sv[h, rows, :] + g * g * now)
                made[2, rows, lane(h)] = ap[h, rows, :] * prefix
                made[4, rows, lane(h)] = sm[h, rows, :] * prefix + g * pull
                made[5, rows, lane(h)] = g * suffix
                g = small[6, h, at, :]
                now = small[7, h, at, :] + g * g * now
        for i in (2, 4, 5, 6):
            put(i).start()

    for yr in range(4):
        pltpu.make_async_copy(bas.at[yr], bas.at[yr], bas_sem.at[yr]).wait()

    obs_wait(0, 2)
    obs_wait(2, 2)

    def farthest(i, carry):
        j = sub_block(i)
        far(0, j)
        far(2, j)
        obs_wait(1, j)
        far(1, j)
        return carry

    lax.fori_loop(0, 4, farthest, 0)
    for part in (0, 2):
        for slot in (1, 3, 0):
            obs_wait(part, slot)

    def round_of(i, carry):
        @pl.when(i < 4)
        def _():
            j = sub_block(i)
            for part in TURNS:
                rest(part, j)
            for part in TURNS:
                send(part, 0, 2, j, relayed=0)
                send(part, 0, 5, j, relayed=1)

        pl.when(i == 0)(variances)
        pl.when(i == 1)(smoother)
        pl.when(i == 2)(weights)

        @pl.when((i >= 1) & (i < 4))
        def _():
            j = sub_block(i - 1)
            for part in TURNS:
                finish(part, (0,), j)

                @pl.when(i == 1)
                def _():
                    send(part, 1, 0)
                    send(part, 1, 1)

                @pl.when(i == 2)
                def _():
                    send(part, 1, 3)
                    send(part, 1, 2, relayed=0)

                @pl.when(i == 3)
                def _():
                    send(part, 1, 4)
                    send(part, 1, 5, relayed=1)

        return carry

    lax.fori_loop(0, 4, round_of, 0)

    for part in TURNS:
        finish(part, (0, 1))
        for message in (0, 1, 3, 4):
            send(part, 2, message)
    for part in TURNS:
        send(part, 2, 2, relayed=0)
        send(part, 2, 5, relayed=1)
    for part in TURNS:
        finish(part, (2,))
        rows = slice(START[part], START[part] + UNIT[part])
        block = acc[part][0 : UNIT[part], :]
        made[0, rows, :] = block
        for h in range(2):
            cc[h, rows, :] = block[:, lane(h)] * kk[h, rows, :]
    put(0).start()

    for h in range(2):
        pv, r = pv_ref[:, lane(h)], r_ref[:, lane(h)]
        retain = (r + (1.0 - flag[0:1, :]) * pv) / (pv + r)
        cc[h, 0:1, :] = cc[h, 0:1, :] + jnp.where(first, retain * pm_ref[:, lane(h)], 0.0)

    def mean_forward(s, carry):
        out = []
        for (g, h), m in zip(blocks, carry):
            m = aa[h, steps(s, g), :] * m + cc[h, steps(s, g), :]
            ll[h, steps(s, g), :] = m
            out.append(m)
        return tuple(out)

    tails = lax.fori_loop(0, 16, mean_forward, (nil,) * 4, unroll=4)

    def mean_backward(i, carry):
        s = 15 - i
        out = []
        for (g, h), m in zip(blocks, carry):
            m = gg[h, steps(s, g), :] * m + ww[h, steps(s, g), :] * ll[h, steps(s, g), :]
            s0[h, steps(s, g), :] = m
            out.append(m)
        return tuple(out)

    fronts = lax.fori_loop(0, 16, mean_backward, (nil,) * 4, unroll=4)
    into, back = ([None] * 16, [None] * 16), ([None] * 16, [None] * 16)
    for h in range(2):
        m, s = zero, zero
        for k in range(16):
            into[h][k] = m
            m = small[4, h, k : k + 1, :] * m + tails[k // 8 * 2 + h][k % 8 : k % 8 + 1]
        for k in range(15, -1, -1):
            back[h][k] = s
            front = fronts[k // 8 * 2 + h][k % 8 : k % 8 + 1]
            s = front + small[5, h, k : k + 1, :] * into[h][k] + small[6, h, k : k + 1, :] * s
        e3[0:1, lane(h)], e3[1:2, lane(h)] = m, s
    scatter(2, e3, g3)
    for h in range(2):
        for k in range(16):
            rows = slice(k * 16, k * 16 + 16)
            made[1, rows, lane(h)] = ll[h, rows, :] + ap[h, rows, :] * into[h][k]
            made[3, rows, lane(h)] = s0[h, rows, :] + sm[h, rows, :] * into[h][k] + gs[h, rows, :] * back[h][k]
    put(1).start()
    put(3).start()
    for part in range(3):
        u = UNIT[part]
        for stage, (begin, rows, base, count) in enumerate(
            ((16 * u, 48 * u, 0, 24), (4 * u, 12 * u, 24, 6), (u, 3 * u, 30, 6))
        ):
            some = quant[part].at[pl.ds(begin, rows)]
            pltpu.make_async_copy(some, some, send_sem.at[part, stage]).wait()
            some = scale_out.at[pl.ds(part * 36 + base, count)]
            pltpu.make_async_copy(some, some, ssend_sem.at[part, stage]).wait()
    for part, slot in tasks:
        to = held[part].at[slot, :, :, pl.ds(0, 512)]
        pltpu.make_async_copy(to, to, psend_sem.at[part, slot]).wait()
    gathered_wait(0, g1, esend_sem)
    gathered_wait(1, g2, esend_sem)
    gathered_wait(2, g3, esend_sem)
    gathered_wait(2, g3, erecv_sem)
    m_in, s_in = [jnp.zeros((1, 256), F32)] * 4, [jnp.zeros((1, 256), F32)] * 4
    for k in range(32):
        left, right = g3[k, 0:1, :], g3[k, 1:2, :]
        m_in[k % 4] = m_in[k % 4] + wm[k] * left
        s_in[k % 4] = s_in[k % 4] + (ws[k] * right + wl[k] * left)
    last[0:1, :] = (m_in[0] + m_in[1]) + (m_in[2] + m_in[3])
    last[1:2, :] = (s_in[0] + s_in[1]) + (s_in[2] + s_in[3])
    put(7).start()
    for i in range(8):
        put(i).wait()


def apply_starts(*refs):
    ins, outs, (got, start, into, back, in_sem, out_sem) = refs[:8], refs[8:12], refs[12:]

    def take(i):
        return pltpu.make_async_copy(ins[i], start if i == 7 else got.at[i], in_sem.at[i])

    def give(i):
        source = (got.at[0], into, back, got.at[6])[i]
        return pltpu.make_async_copy(source, outs[i], out_sem.at[i])

    order = (7, 1, 2, 3, 4, 5, 0, 6)
    for i in order:
        take(i).start()
    for i in (7, 1, 2):
        take(i).wait()
    m_in, s_in = start[0:1, :], start[1:2, :]
    into[...] = got[1] + got[2] * m_in
    give(1).start()
    for i in (3, 4, 5):
        take(i).wait()
    back[...] = got[3] + got[4] * m_in + got[5] * s_in
    give(2).start()
    take(0).wait()
    give(0).start()
    take(6).wait()
    give(3).start()
    for i in range(4):
        give(i).wait()


def body(observations, pod_basis, decay, step_mask, process_var, obs_var, prior_mean, prior_var):
    block = jax.ShapeDtypeStruct((256, 256), F32)
    vmem = pl.BlockSpec(memory_space=pltpu.VMEM)
    anywhere = pl.BlockSpec(memory_space=pl.ANY)
    plane = pltpu.VMEM((2, 256, 128), F32)
    landing = [
        pltpu.VMEM(shape, I16) for u in UNIT for shape in ((24, 2 * u, 256), (6, 2 * u, 256), (6, u // 2, 256))
    ]
    dma = pltpu.SemaphoreType.DMA
    scratch = [
        pltpu.VMEM((7, 256, 256), F32),
        pltpu.VMEM((2, 256), F32),
        dma((8,)),
        *[pltpu.VMEM((rows, 256), F32) for rows in ROWS],
        *[pltpu.VMEM((rows, 256), I16) for rows in ROWS],
        *landing,
        *[pltpu.VMEM((4, 4, u, 1024), BF16) for u in UNIT],
        pltpu.VMEM((4, 1024, 256), BF16),
        pltpu.VMEM((108, 1, 256), F32),
        pltpu.VMEM((108, 1, 256), F32),
        pltpu.VMEM((2, 288, 128), F32),
        pltpu.VMEM((256, 128), F32),
        *[plane] * 13,
        pltpu.VMEM((14, 2, 16, 128), F32),
        pltpu.VMEM((4, 256), F32),
        pltpu.VMEM((4, 256), F32),
        pltpu.VMEM((2, 256), F32),
        pltpu.VMEM((32, 4, 256), F32),
        pltpu.VMEM((32, 4, 256), F32),
        pltpu.VMEM((32, 2, 256), F32),
        *[pltpu.VMEM((32, 1, 256), F32)] * 3,
        dma((3, 4)),
        dma((3, 4)),
        dma((3, 4)),
        dma((4,)),
        dma((3, 3)),
        dma((108,)),
        dma((3, 3)),
        dma((108,)),
        dma((3,)),
        dma((3,)),
    ]
    made = pl.pallas_call(
        kernel,
        out_shape=[block] * 7 + [jax.ShapeDtypeStruct((2, 256), F32)],
        in_specs=[anywhere, anywhere, *[vmem] * 6],
        out_specs=[anywhere] * 8,
        scratch_shapes=scratch,
        compiler_params=pltpu.CompilerParams(
            collective_id=0, has_side_effects=True, vmem_limit_bytes=60 * 2**20
        ),
    )(
        observations.reshape(4, 4, 2, 256, 512),
        pod_basis.reshape(32, 512, 1024),
        decay,
        step_mask.reshape(1, 256),
        process_var.reshape(1, 256),
        obs_var.reshape(1, 256),
        prior_mean.reshape(1, 256),
        prior_var.reshape(1, 256),
    )
    return tuple(
        pl.pallas_call(
            apply_starts,
            out_shape=[block] * 4,
            in_specs=[anywhere] * 8,
            out_specs=[anywhere] * 4,
            scratch_shapes=[
                pltpu.VMEM((7, 256, 256), F32),
                pltpu.VMEM((2, 256), F32),
                pltpu.VMEM((256, 256), F32),
                pltpu.VMEM((256, 256), F32),
                dma((8,)),
                dma((4,)),
            ],
            compiler_params=pltpu.CompilerParams(vmem_limit_bytes=60 * 2**20),
        )(*made)
    )


def solution(mesh):
    return jax.shard_map(
        body,
        mesh=mesh,
        in_specs=(
            P(None, "tm", "space", None),
            P(None, "space", None, None),
            P("tm", "space"),
            P("tm"),
            P("space"),
            P("space"),
            P("space"),
            P("space"),
        ),
        out_specs=(P("tm", "space"), P("tm", "space"), P("tm", "space"), P("tm", "space")),
        check_vma=False,
    )
```

```python
import functools

import jax
import jax.numpy as jnp
from jax import lax
from jax.experimental import pallas as pl
from jax.experimental.pallas import tpu as pltpu
from jax.sharding import PartitionSpec as P

MESH = pl.DeviceIdType.MESH
F32 = jnp.float32
BF16 = jnp.bfloat16
I16 = jnp.int16

UNIT = (96, 64, 96)
START = (0, 96, 160)
ORDER = (("x", "y", "z"), ("y", "z", "x"), ("z", "y", "x"))
ROWS = tuple(64 * u for u in UNIT)
LIMIT = 32760.0
TINY = 1e-33
TURNS = (0, 2, 1)

MESSAGES = ((2, 0, 1), (2, 1, -1), (1, 0, 1), (1, 1, 1), (3, 0, -1), (3, 1, -1))


def turn(value, by, count):
    return lax.rem(value + by, count)


def sub_block(i):
    return lax.rem(2 + 3 * i + 3 * (i // 2) + 2 * (i // 3), 4)


def lane(h):
    return slice(h * 128, h * 128 + 128)


def kernel(obs, basis, decay, mask, q_ref, r_ref, pm_ref, pv_ref, *refs):
    outs, scratch = refs[:8], refs[8:]
    (made, last, made_sem, fa, fb, fc, qa, qb, qc, ra1, ra2, ra3, rb1, rb2, rb3, rc1, rc2, rc3, oa, ob, oc, bas, scale_out, scale_in,
     dec, flag, qv, vv, aa, kk, gg, ww, ap, sm, gs, sv, cc, ll, s0, al, be, small, e1, e2, e3, g1, g2, g3, wm, ws, wl,
     own_sem, part_sem, psend_sem, bas_sem, send_sem, recv_sem, ssend_sem, srecv_sem, esend_sem, erecv_sem) = scratch
    def put(i):
        source = last if i == 7 else made.at[i]
        return pltpu.make_async_copy(source, outs[i], made_sem.at[i])

    acc = (fa, fb, fc)
    quant = (qa, qb, qc)
    landed = ((ra1, ra2, ra3), (rb1, rb2, rb3), (rc1, rc2, rc3))
    held = (oa, ob, oc)
    tm = lax.axis_index("tm")
    y = lax.axis_index("space")
    x, z, core = tm // 8, lax.rem(tm // 2, 4), lax.rem(tm, 2)
    partner = tm + 1 - 2 * core

    def neighbour(axis, way):
        if axis == "x":
            return {"tm": turn(tm, 8 if way > 0 else 24, 32)}
        if axis == "z":
            return {"tm": x * 8 + turn(z, 1 if way > 0 else 3, 4) * 2 + core}
        return {"space": turn(y, 1 if way > 0 else 3, 4)}

    barrier = pltpu.get_barrier_semaphore()

    def greet(step, carry):
        pl.semaphore_signal(barrier, inc=1, device_id={"tm": turn(tm, step, 32)}, device_id_type=MESH)
        return carry

    lax.fori_loop(1, 32, greet, 0)
    for way in (1, -1):
        pl.semaphore_signal(barrier, inc=1, device_id=neighbour("y", way), device_id_type=MESH)

    def obs_copies(part, slot):
        rows = slice(START[part], START[part] + UNIT[part])
        pieces = []
        for other in range(4):
            at = (turn(x, slot, 4), turn(z, other, 4)) if part == 0 else (turn(x, other, 4), turn(z, slot, 4))
            pieces.append((at, rows, held[part].at[slot, other]))
        return pieces

    tasks = [(0, 2), (2, 2), (1, 2), (1, 1), (1, 3), (1, 0), (0, 1), (0, 3), (0, 0), (2, 1), (2, 3), (2, 0)]
    for yr in (2, 1, 3, 0):
        columns = pl.ds(pl.multiple_of(turn(y, yr, 4) * 256, 256), 256)
        for side, who in ((0, tm), (1, partner)):
            pltpu.make_async_copy(
                basis.at[who, :, columns], bas.at[yr, pl.ds(side * 512, 512)], bas_sem.at[yr]
            ).start()
    for part, slot in tasks:
        for (xi, zi), rows, to in obs_copies(part, slot):
            pltpu.make_async_copy(obs.at[xi, zi, core, rows], to.at[:, 0:512], own_sem.at[part, slot]).start()

    first = tm == 0
    for h in range(2):
        dec[h, 0:256, :] = decay[:, lane(h)]
        e1[3:4, lane(h)] = dec[h, 0:1, :]
        qv[h] = jnp.broadcast_to(q_ref[:, lane(h)], (256, 128))
        qv[h, 0:1, :] = jnp.where(first, pv_ref[:, lane(h)], q_ref[:, lane(h)])
        dec[h, 0:1, :] = jnp.where(first, 0.0, dec[h, 0:1, :])
    row = lax.broadcasted_iota(jnp.int32, (256, 256), 0)
    column = lax.broadcasted_iota(jnp.int32, (256, 256), 1)
    spread_mask = jnp.where(row == column, jnp.broadcast_to(mask[...].astype(F32), (256, 256)), 0.0).astype(BF16)
    flag[...] = jnp.dot(spread_mask, jnp.ones((256, 128), BF16), preferred_element_type=F32)

    def wide(ref, h):
        return jnp.broadcast_to(ref[:, lane(h)], (8, 128))

    blocks = [(g, h) for g in range(2) for h in range(2)]

    def steps(s, g):
        return pl.ds(g * 128 + s, 8, stride=16)

    def join(early, late):
        lead_e, spread_e, weight_e = early
        lead_l, spread_l, weight_l = late
        factor = 1.0 / (1.0 + spread_e * weight_l)
        return (
            lead_l * factor * lead_e,
            lead_l * lead_l * factor * spread_e + spread_l,
            lead_e * lead_e * factor * weight_l + weight_e,
        )

    def compose(s, carry):
        out = []
        for (g, h), early in zip(blocks, carry):
            seen, d, q = flag[steps(s, g), :], dec[h, steps(s, g), :], qv[h, steps(s, g), :]
            noise = wide(r_ref, h)
            den = 1.0 / (q + noise)
            retain = (noise + (1.0 - seen) * q) * den
            out.append(join(early, (retain * d, retain * q, seen * d * d * den)))
        return tuple(out)

    one, nil = jnp.ones((8, 128), F32), jnp.zeros((8, 128), F32)
    unit, zero = jnp.ones((1, 128), F32), jnp.zeros((1, 128), F32)
    chunks = lax.fori_loop(0, 16, compose, ((one, nil, nil),) * 4, unroll=2)
    totals = []
    for (g, h), parts in zip(blocks, chunks):
        for i in range(3):
            small[i, h, g * 8 : g * 8 + 8, :] = parts[i]
        totals.append(tuple(part[0:1] for part in parts))
    for k in range(1, 8):
        totals = [join(t, tuple(p[k : k + 1] for p in parts)) for t, parts in zip(totals, chunks)]
    for h in range(2):
        for i, value in enumerate(join(totals[h], totals[2 + h])):
            e1[i : i + 1, lane(h)] = value
        for i in range(3):
            small[11 + i, h, 0:1, :] = totals[h][i]

    pl.semaphore_wait(barrier, 33)

    def exchange(*pieces):
        for part, slot in pieces:
            for (xi, zi), rows, to in obs_copies(part, slot):
                pltpu.make_async_remote_copy(
                    obs.at[xi, zi, 1 - core, rows],
                    to.at[:, 512:1024],
                    psend_sem.at[part, slot],
                    part_sem.at[part, slot],
                    device_id={"tm": partner},
                    device_id_type=MESH,
                ).start()

    exchange(*tasks)

    def scatter(number, mine, gathered):
        gathered[tm] = mine[...]

        def push(step, carry):
            pltpu.make_async_remote_copy(
                mine,
                gathered.at[tm],
                esend_sem.at[number],
                erecv_sem.at[number],
                device_id={"tm": turn(tm, step, 32)},
                device_id_type=MESH,
            ).start()
            return carry

        lax.fori_loop(1, 32, push, 0)

    def gathered_wait(number, gathered, sem):
        some = gathered.at[pl.ds(0, 31)]
        pltpu.make_async_copy(some, some, sem.at[number]).wait()

    scatter(0, e1, g1)

    def obs_wait(part, slot):
        to = held[part].at[slot, :, :, pl.ds(0, 512)]
        pltpu.make_async_copy(to, to, own_sem.at[part, slot]).wait()
        pltpu.make_async_copy(to, to, part_sem.at[part, slot]).wait()

    def product(part, slot, j):
        u = UNIT[part]
        obs_slot, mode_slot = (j, slot) if part == 1 else (slot, j if part == 0 else lax.rem(4 - j, 4))
        return jnp.dot(held[part][obs_slot].reshape(4 * u, 1024), bas[mode_slot], preferred_element_type=F32)

    def place(part, stage, message, j):
        slot, half, _ = MESSAGES[message]
        u = UNIT[part]
        if stage == 0:
            return (slot * 4 + j) * (4 * u) + half * (2 * u), 2 * u
        if stage == 1:
            return slot * 4 * u + half * 2 * u, 2 * u
        return slot * u + half * (u // 2), u // 2

    def number_of(part, stage, message, j):
        return part * 36 + (j * 6 if stage == 0 else 18 + 6 * stage) + message

    def index_of(stage, message, j):
        return j * 6 + message if stage == 0 else message

    def peak(block):
        return jnp.max(jnp.abs(block).reshape(-1, 8, 256), axis=0)

    def steps_of(top):
        top = jnp.maximum(jnp.max(top, axis=0, keepdims=True), TINY)
        return top * (1.0 / LIMIT), LIMIT / top

    def copies(part, stage, message, j):
        begin, rows = place(part, stage, message, j)
        to = neighbour(ORDER[part][stage], -MESSAGES[message][2] if (part, stage) == (2, 1) else MESSAGES[message][2])
        number = number_of(part, stage, message, j)
        return (
            pltpu.make_async_remote_copy(
                quant[part].at[pl.ds(pl.multiple_of(begin, 16), rows)],
                landed[part][stage].at[index_of(stage, message, j)],
                send_sem.at[part, stage],
                recv_sem.at[number],
                device_id=to,
                device_id_type=MESH,
            ),
            pltpu.make_async_remote_copy(
                scale_out.at[number],
                scale_in.at[number],
                ssend_sem.at[part, stage],
                srecv_sem.at[number],
                device_id=to,
                device_id_type=MESH,
            ),
        )

    def recv_wait(part, stage, message, j):
        for copy in copies(part, stage, message, j):
            copy.wait_recv()

    def send(part, stage, message, j=0, relayed=None):
        begin, rows = place(part, stage, message, j)
        number = number_of(part, stage, message, j)
        size = min(rows, 64)
        if relayed is not None:
            recv_wait(part, stage, relayed, j)
            factor = scale_in[number_of(part, stage, relayed, j)]

        def measure(k, top):
            at = pl.ds(pl.multiple_of(begin + k * size, 16), size)
            block = acc[part][at, :]
            if relayed is not None:
                came = landed[part][stage][index_of(stage, relayed, j), pl.ds(pl.multiple_of(k * size, 16), size), :]
                block = block + came.astype(F32) * factor
                acc[part][at, :] = block
            return jnp.maximum(top, peak(block))

        top = lax.fori_loop(0, rows // size, measure, jnp.zeros((8, 256), F32))
        scale_out[number], inverse = steps_of(top)

        def encode(k, carry):
            at = pl.ds(pl.multiple_of(begin + k * size, 16), size)
            quant[part][at, :] = jnp.round(acc[part][at, :] * inverse).astype(I16)
            return carry

        lax.fori_loop(0, rows // size, encode, 0)
        for copy in copies(part, stage, message, j):
            copy.start()

    def far(part, j):
        total = product(part, 2, j)
        u = UNIT[part]
        for message in (0, 1):
            begin, rows = place(part, 0, message, j)
            block = total[message * 2 * u : message * 2 * u + 2 * u]
            scale_out[number_of(part, 0, message, j)], inverse = steps_of(peak(block))
            at = pl.ds(pl.multiple_of(begin, 16), rows)
            quant[part][at, :] = jnp.round(block * inverse).astype(I16)
            for copy in copies(part, 0, message, j):
                copy.start()

    def rest(part, j):
        u = UNIT[part]

        def block(k, carry):
            slot = lax.rem(1 + 2 * k + 3 * (k // 2), 4)
            acc[part][pl.ds(pl.multiple_of((slot * 4 + j) * (4 * u), 16), 4 * u), :] = product(part, slot, j)
            return carry

        lax.fori_loop(0, 3, block, 0)
        send(part, 0, 3, j)
        send(part, 0, 4, j)

    def finish(part, stages, j=0):
        u = UNIT[part]
        rows = u // 2 if stages == (2,) else 2 * u
        size = min(rows, 64)
        for half, pair in enumerate(((2, 4), (3, 5))):
            begin = half * rows + (j * (4 * u) if stages == (0,) else 0)
            came = [(stage, message) for stage in stages for message in pair]
            for stage, message in came:
                recv_wait(part, stage, message, j)
            scales = [scale_in[number_of(part, stage, m, j)] for stage, m in came]

            def add(k, carry):
                at = pl.ds(pl.multiple_of(begin + k * size, 16), size)
                block = acc[part][at, :]
                for (stage, m), factor in zip(came, scales):
                    rows_in = pl.ds(pl.multiple_of(k * size, 16), size)
                    block = block + landed[part][stage][index_of(stage, m, j), rows_in, :].astype(F32) * factor
                acc[part][at, :] = block
                return carry

            lax.fori_loop(0, rows // size, add, 0)

    def variances():
        gathered_wait(0, g1, erecv_sem)

        def enter(k, v):
            lead, spread, weight = (g1[k, i : i + 1, :] for i in range(3))
            return jnp.where(k < tm, lead * lead * v / (1.0 + weight * v) + spread, v)

        v = lax.fori_loop(0, 31, enter, jnp.zeros((1, 256), F32), unroll=2)
        after = turn(tm, 1, 32)
        now = []
        for h in range(2):
            dec[h, 256:257, :] = jnp.where(tm == 31, 0.0, g1[after, 3:4, lane(h)])
            now.append(v[:, lane(h)])
        for h in range(2):
            lead, spread, weight = (small[11 + i, h, 0:1, :] for i in range(3))
            now.append(lead * lead * now[h] / (1.0 + weight * now[h]) + spread)
        for k in range(8):
            for b, (g, h) in enumerate(blocks):
                at = slice(g * 8 + k, g * 8 + k + 1)
                small[3, h, at, :] = now[b]
                if k < 7:
                    lead, spread, weight = (small[i, h, at, :] for i in range(3))
                    now[b] = lead * lead * now[b] / (1.0 + weight * now[b]) + spread

        def forward(s, carry):
            out = []
            for (g, h), (v, prefix) in zip(blocks, carry):
                seen, d, q = flag[steps(s, g), :], dec[h, steps(s, g), :], qv[h, steps(s, g), :]
                noise = wide(r_ref, h)
                vp = d * d * v + q
                den = 1.0 / (vp + noise)
                retain = (noise + (1.0 - seen) * vp) * den
                v = retain * vp
                a = retain * d
                prefix = prefix * a
                vv[h, steps(s, g), :] = v
                aa[h, steps(s, g), :] = a
                kk[h, steps(s, g), :] = seen * vp * den
                ap[h, steps(s, g), :] = prefix
                out.append((v, prefix))
            return tuple(out)

        starts = tuple((small[3, h, g * 8 : g * 8 + 8, :], one) for g, h in blocks)
        ends = lax.fori_loop(0, 16, forward, starts, unroll=2)
        for (g, h), (_, prefix) in zip(blocks, ends):
            small[4, h, g * 8 : g * 8 + 8, :] = prefix

    def smoother():
        def backward(i, carry):
            s = 15 - i
            out = []
            for (g, h), (var, pull, suffix) in zip(blocks, carry):
                nd, v = dec[h, steps(s + 1, g), :], vv[h, steps(s, g), :]
                process = wide(q_ref, h)
                inverse = 1.0 / (nd * nd * v + process)
                gain, w = v * nd * inverse, process * inverse
                var = gain * gain * var + v * w
                pull = gain * pull + w * ap[h, steps(s, g), :]
                suffix = gain * suffix
                gg[h, steps(s, g), :] = gain
                ww[h, steps(s, g), :] = w
                sv[h, steps(s, g), :] = var
                sm[h, steps(s, g), :] = pull
                gs[h, steps(s, g), :] = suffix
                out.append((var, pull, suffix))
            return tuple(out)

        heads = lax.fori_loop(0, 16, backward, ((nil, nil, one),) * 4, unroll=2)
        for (g, h), (var, pull, suffix) in zip(blocks, heads):
            rows = slice(g * 8, g * 8 + 8)
            small[5, h, rows, :], small[6, h, rows, :], small[7, h, rows, :] = pull, suffix, var
        for h in range(2):
            m = unit
            for k in range(16):
                small[8, h, k : k + 1, :] = m
                m = m * small[4, h, k : k + 1, :]
            e2[0:1, lane(h)] = m
            s_var, s_pull, s_suffix = zero, zero, unit
            for k in range(15, -1, -1):
                at = slice(k, k + 1)
                small[9, h, at, :], small[10, h, at, :] = s_pull, s_suffix
                g = small[6, h, at, :]
                s_var = small[7, h, at, :] + g * g * s_var
                s_pull = small[5, h, at, :] * small[8, h, at, :] + g * s_pull
                s_suffix = g * s_suffix
            e2[1:2, lane(h)], e2[2:3, lane(h)], e2[3:4, lane(h)] = s_pull, s_suffix, s_var
        scatter(1, e2, g2)

    def weights():
        gathered_wait(1, g2, erecv_sem)

        def down(i, carry):
            k = 31 - i
            var, w = carry
            prefix, suffix, spread = g2[k, 0:1, :], g2[k, 2:3, :], g2[k, 3:4, :]
            wm[k] = jnp.where(k < tm, w, 0.0)
            return (
                jnp.where(k > tm, spread + suffix * suffix * var, var),
                jnp.where(k < tm, prefix * w, w),
            )

        var, _ = lax.fori_loop(0, 32, down, (jnp.zeros((1, 256), F32), jnp.ones((1, 256), F32)), unroll=2)

        def up(k, w):
            ws[k] = jnp.where(k > tm, w, 0.0)
            return jnp.where(k > tm, g2[k, 2:3, :] * w, w)

        lax.fori_loop(0, 32, up, jnp.ones((1, 256), F32), unroll=2)

        def across(i, pull):
            k = 31 - i
            wl[k] = pull
            return ws[k] * g2[k, 1:2, :] + g2[k, 0:1, :] * pull

        lax.fori_loop(0, 32, across, jnp.zeros((1, 256), F32), unroll=2)
        for h in range(2):
            now = var[:, lane(h)]
            for k in range(15, -1, -1):
                rows, at = slice(k * 16, k * 16 + 16), slice(k, k + 1)
                g = gs[h, rows, :]
                prefix, pull, suffix = (small[i, h, at, :] for i in (8, 9, 10))
                made[6, rows, lane(h)] = jnp.log(sv[h, rows, :] + g * g * now)
                made[2, rows, lane(h)] = ap[h, rows, :] * prefix
                made[4, rows, lane(h)] = sm[h, rows, :] * prefix + g * pull
                made[5, rows, lane(h)] = g * suffix
                g = small[6, h, at, :]
                now = small[7, h, at, :] + g * g * now
        for i in (2, 4, 5, 6):
            put(i).start()

    def functionals():
        def gains_before(s, carry):
            out = []
            for (g, h), gamma in zip(blocks, carry):
                s0[h, steps(s, g), :] = gamma * ww[h, steps(s, g), :]
                out.append(gamma * gg[h, steps(s, g), :])
            return tuple(out)

        lax.fori_loop(0, 16, gains_before, (one,) * 4, unroll=2)

        def effects(i, carry):
            s = 15 - i
            out = []
            for (g, h), (after, effect) in zip(blocks, carry):
                a = aa[h, steps(s, g), :]
                effect = s0[h, steps(s, g), :] + effect
                al[h, steps(s, g), :] = after
                be[h, steps(s, g), :] = effect
                out.append((after * a, effect * a))
            return tuple(out)

        lax.fori_loop(0, 16, effects, ((one, nil),) * 4, unroll=2)
        for h in range(2):
            gamma, gammas = unit, []
            for k in range(16):
                gammas.append(gamma)
                gamma = gamma * small[6, h, k : k + 1, :]
            onward, pull = unit, zero
            for k in range(15, -1, -1):
                rows, at = slice(k * 16, k * 16 + 16), slice(k, k + 1)
                after = al[h, rows, :]
                left, right = after * onward, gammas[k] * be[h, rows, :] + after * pull
                if k == 0:
                    small[14, h, 0:1, :], small[15, h, 0:1, :] = left[0:1], right[0:1]
                al[h, rows, :] = left * kk[h, rows, :]
                be[h, rows, :] = right * kk[h, rows, :]
                pull = gammas[k] * small[5, h, at, :] + small[4, h, at, :] * pull
                onward = onward * small[4, h, at, :]

    for yr in range(4):
        pltpu.make_async_copy(bas.at[yr], bas.at[yr], bas_sem.at[yr]).wait()

    obs_wait(0, 2)
    obs_wait(2, 2)

    def farthest(i, carry):
        j = sub_block(i)
        far(0, j)
        far(2, j)
        obs_wait(1, j)
        far(1, j)
        return carry

    lax.fori_loop(0, 4, farthest, 0)
    for part in (0, 2):
        for slot in (1, 3, 0):
            obs_wait(part, slot)

    def round_of(i, carry):
        @pl.when(i < 4)
        def _():
            j = sub_block(i)
            for part in TURNS:
                rest(part, j)
            for part in TURNS:
                send(part, 0, 2, j, relayed=0)
                send(part, 0, 5, j, relayed=1)

        pl.when(i == 0)(variances)
        pl.when(i == 1)(smoother)

        @pl.when((i >= 1) & (i < 4))
        def _():
            j = sub_block(i - 1)
            for part in TURNS:
                finish(part, (0,), j)

                @pl.when(i == 1)
                def _():
                    send(part, 1, 0)
                    send(part, 1, 1)

                @pl.when(i == 2)
                def _():
                    send(part, 1, 3)
                    send(part, 1, 2, relayed=0)

                @pl.when(i == 3)
                def _():
                    send(part, 1, 4)
                    send(part, 1, 5, relayed=1)

        return carry

    lax.fori_loop(0, 4, round_of, 0)
    weights()
    functionals()

    for part in TURNS:
        finish(part, (0, 1))
        for message in (0, 1, 3, 4):
            send(part, 2, message)
    for part in TURNS:
        send(part, 2, 2, relayed=0)
        send(part, 2, 5, relayed=1)
    ends, heads = [nil, nil], [nil, nil]
    for part in TURNS:
        finish(part, (2,))
        rows = slice(START[part], START[part] + UNIT[part])
        block = acc[part][0 : UNIT[part], :]
        made[0, rows, :] = block
        for h in range(2):
            half = block[:, lane(h)]
            cc[h, rows, :] = half * kk[h, rows, :]
            ends[h] = ends[h] + jnp.sum((half * al[h, rows, :]).reshape(-1, 8, 128), axis=0)
            heads[h] = heads[h] + jnp.sum((half * be[h, rows, :]).reshape(-1, 8, 128), axis=0)

    for h in range(2):
        pv, r = pv_ref[:, lane(h)], r_ref[:, lane(h)]
        retain = (r + (1.0 - flag[0:1, :]) * pv) / (pv + r)
        prior = jnp.where(first, retain * pm_ref[:, lane(h)], 0.0)
        cc[h, 0:1, :] = cc[h, 0:1, :] + prior
        e3[0:1, lane(h)] = jnp.sum(ends[h], axis=0, keepdims=True) + small[14, h, 0:1, :] * prior
        e3[1:2, lane(h)] = jnp.sum(heads[h], axis=0, keepdims=True) + small[15, h, 0:1, :] * prior
    scatter(2, e3, g3)
    put(0).start()

    def mean_forward(s, carry):
        out = []
        for (g, h), m in zip(blocks, carry):
            m = aa[h, steps(s, g), :] * m + cc[h, steps(s, g), :]
            ll[h, steps(s, g), :] = m
            out.append(m)
        return tuple(out)

    tails = lax.fori_loop(0, 16, mean_forward, (nil,) * 4, unroll=4)

    def mean_backward(i, carry):
        s = 15 - i
        out = []
        for (g, h), m in zip(blocks, carry):
            m = gg[h, steps(s, g), :] * m + ww[h, steps(s, g), :] * ll[h, steps(s, g), :]
            s0[h, steps(s, g), :] = m
            out.append(m)
        return tuple(out)

    fronts = lax.fori_loop(0, 16, mean_backward, (nil,) * 4, unroll=4)
    into, back = ([None] * 16, [None] * 16), ([None] * 16, [None] * 16)
    for h in range(2):
        m, s = zero, zero
        for k in range(16):
            into[h][k] = m
            m = small[4, h, k : k + 1, :] * m + tails[k // 8 * 2 + h][k % 8 : k % 8 + 1]
        for k in range(15, -1, -1):
            back[h][k] = s
            front = fronts[k // 8 * 2 + h][k % 8 : k % 8 + 1]
            s = front + small[5, h, k : k + 1, :] * into[h][k] + small[6, h, k : k + 1, :] * s
    for h in range(2):
        for k in range(16):
            rows = slice(k * 16, k * 16 + 16)
            made[1, rows, lane(h)] = ll[h, rows, :] + ap[h, rows, :] * into[h][k]
            made[3, rows, lane(h)] = s0[h, rows, :] + sm[h, rows, :] * into[h][k] + gs[h, rows, :] * back[h][k]
    put(1).start()
    put(3).start()
    for part in range(3):
        u = UNIT[part]
        for stage, (begin, rows, base, count) in enumerate(
            ((16 * u, 48 * u, 0, 24), (4 * u, 12 * u, 24, 6), (u, 3 * u, 30, 6))
        ):
            some = quant[part].at[pl.ds(begin, rows)]
            pltpu.make_async_copy(some, some, send_sem.at[part, stage]).wait()
            some = scale_out.at[pl.ds(part * 36 + base, count)]
            pltpu.make_async_copy(some, some, ssend_sem.at[part, stage]).wait()
    for part, slot in tasks:
        to = held[part].at[slot, :, :, pl.ds(0, 512)]
        pltpu.make_async_copy(to, to, psend_sem.at[part, slot]).wait()
    gathered_wait(0, g1, esend_sem)
    gathered_wait(1, g2, esend_sem)
    gathered_wait(2, g3, esend_sem)
    gathered_wait(2, g3, erecv_sem)
    m_in, s_in = [jnp.zeros((1, 256), F32)] * 4, [jnp.zeros((1, 256), F32)] * 4
    for k in range(32):
        left, right = g3[k, 0:1, :], g3[k, 1:2, :]
        m_in[k % 4] = m_in[k % 4] + wm[k] * left
        s_in[k % 4] = s_in[k % 4] + (ws[k] * right + wl[k] * left)
    last[0:1, :] = (m_in[0] + m_in[1]) + (m_in[2] + m_in[3])
    last[1:2, :] = (s_in[0] + s_in[1]) + (s_in[2] + s_in[3])
    put(7).start()
    for i in range(8):
        put(i).wait()


def apply_starts(*refs):
    ins, outs, (got, start, into, back, in_sem, out_sem) = refs[:8], refs[8:12], refs[12:]

    def take(i):
        return pltpu.make_async_copy(ins[i], start if i == 7 else got.at[i], in_sem.at[i])

    def give(i):
        source = (got.at[0], into, back, got.at[6])[i]
        return pltpu.make_async_copy(source, outs[i], out_sem.at[i])

    order = (7, 1, 2, 3, 4, 5, 0, 6)
    for i in order:
        take(i).start()
    for i in (7, 1, 2):
        take(i).wait()
    m_in, s_in = start[0:1, :], start[1:2, :]
    into[...] = got[1] + got[2] * m_in
    give(1).start()
    for i in (3, 4, 5):
        take(i).wait()
    back[...] = got[3] + got[4] * m_in + got[5] * s_in
    give(2).start()
    take(0).wait()
    give(0).start()
    take(6).wait()
    give(3).start()
    for i in range(4):
        give(i).wait()


def body(observations, pod_basis, decay, step_mask, process_var, obs_var, prior_mean, prior_var):
    block = jax.ShapeDtypeStruct((256, 256), F32)
    vmem = pl.BlockSpec(memory_space=pltpu.VMEM)
    anywhere = pl.BlockSpec(memory_space=pl.ANY)
    plane = pltpu.VMEM((2, 256, 128), F32)
    landing = [
        pltpu.VMEM(shape, I16) for u in UNIT for shape in ((24, 2 * u, 256), (6, 2 * u, 256), (6, u // 2, 256))
    ]
    dma = pltpu.SemaphoreType.DMA
    scratch = [
        pltpu.VMEM((7, 256, 256), F32),
        pltpu.VMEM((2, 256), F32),
        dma((8,)),
        *[pltpu.VMEM((rows, 256), F32) for rows in ROWS],
        *[pltpu.VMEM((rows, 256), I16) for rows in ROWS],
        *landing,
        *[pltpu.VMEM((4, 4, u, 1024), BF16) for u in UNIT],
        pltpu.VMEM((4, 1024, 256), BF16),
        pltpu.VMEM((108, 1, 256), F32),
        pltpu.VMEM((108, 1, 256), F32),
        pltpu.VMEM((2, 288, 128), F32),
        pltpu.VMEM((256, 128), F32),
        *[plane] * 15,
        pltpu.VMEM((16, 2, 16, 128), F32),
        pltpu.VMEM((4, 256), F32),
        pltpu.VMEM((4, 256), F32),
        pltpu.VMEM((2, 256), F32),
        pltpu.VMEM((32, 4, 256), F32),
        pltpu.VMEM((32, 4, 256), F32),
        pltpu.VMEM((32, 2, 256), F32),
        *[pltpu.VMEM((32, 1, 256), F32)] * 3,
        dma((3, 4)),
        dma((3, 4)),
        dma((3, 4)),
        dma((4,)),
        dma((3, 3)),
        dma((108,)),
        dma((3, 3)),
        dma((108,)),
        dma((3,)),
        dma((3,)),
    ]
    made = pl.pallas_call(
        kernel,
        out_shape=[block] * 7 + [jax.ShapeDtypeStruct((2, 256), F32)],
        in_specs=[anywhere, anywhere, *[vmem] * 6],
        out_specs=[anywhere] * 8,
        scratch_shapes=scratch,
        compiler_params=pltpu.CompilerParams(
            collective_id=0, has_side_effects=True, vmem_limit_bytes=60 * 2**20
        ),
    )(
        observations.reshape(4, 4, 2, 256, 512),
        pod_basis.reshape(32, 512, 1024),
        decay,
        step_mask.reshape(1, 256),
        process_var.reshape(1, 256),
        obs_var.reshape(1, 256),
        prior_mean.reshape(1, 256),
        prior_var.reshape(1, 256),
    )
    return tuple(
        pl.pallas_call(
            apply_starts,
            out_shape=[block] * 4,
            in_specs=[anywhere] * 8,
            out_specs=[anywhere] * 4,
            scratch_shapes=[
                pltpu.VMEM((7, 256, 256), F32),
                pltpu.VMEM((2, 256), F32),
                pltpu.VMEM((256, 256), F32),
                pltpu.VMEM((256, 256), F32),
                dma((8,)),
                dma((4,)),
            ],
            compiler_params=pltpu.CompilerParams(vmem_limit_bytes=60 * 2**20),
        )(*made)
    )


def solution(mesh):
    return jax.shard_map(
        body,
        mesh=mesh,
        in_specs=(
            P(None, "tm", "space", None),
            P(None, "space", None, None),
            P("tm", "space"),
            P("tm"),
            P("space"),
            P("space"),
            P("space"),
            P("space"),
        ),
        out_specs=(P("tm", "space"), P("tm", "space"), P("tm", "space"), P("tm", "space")),
        check_vma=False,
    )
```

```python
import functools

import jax
import jax.numpy as jnp
from jax import lax
from jax.experimental import pallas as pl
from jax.experimental.pallas import tpu as pltpu
from jax.sharding import PartitionSpec as P

MESH = pl.DeviceIdType.MESH
F32 = jnp.float32
BF16 = jnp.bfloat16
I16 = jnp.int16

UNIT = (96, 64, 96)
START = (0, 96, 160)
ORDER = (("x", "y", "z"), ("y", "z", "x"), ("z", "y", "x"))
ROWS = tuple(64 * u for u in UNIT)
LIMIT = 32760.0
TINY = 1e-33
TURNS = (0, 2, 1)

LAST = (2, 1, 3)

MESSAGES = ((2, 0, 1), (2, 1, -1), (1, 0, 1), (1, 1, 1), (3, 0, -1), (3, 1, -1))


def turn(value, by, count):
    return lax.rem(value + by, count)


def sub_block(i):
    return lax.rem(2 + 3 * i + 3 * (i // 2) + 2 * (i // 3), 4)


def lane(h):
    return slice(h * 128, h * 128 + 128)


def kernel(obs, basis, decay, mask, q_ref, r_ref, pm_ref, pv_ref, *refs):
    outs, scratch = refs[:8], refs[8:]
    (made, last, made_sem, fa, fb, fc, qa, qb, qc, ra1, ra2, ra3, rb1, rb2, rb3, rc1, rc2, rc3, oa, ob, oc, bas, scale_out, scale_in,
     dec, flag, qv, vv, aa, kk, gg, ww, ap, sm, gs, sv, cc, ll, s0, al, be, small, e1, e2, e3, g1, g2, g3, wm, ws, wl,
     own_sem, part_sem, psend_sem, bas_sem, send_sem, recv_sem, ssend_sem, srecv_sem, esend_sem, erecv_sem) = scratch
    def put(i):
        source = last if i == 7 else made.at[i]
        return pltpu.make_async_copy(source, outs[i], made_sem.at[i])

    acc = (fa, fb, fc)
    quant = (qa, qb, qc)
    landed = ((ra1, ra2, ra3), (rb1, rb2, rb3), (rc1, rc2, rc3))
    held = (oa, ob, oc)
    tm = lax.axis_index("tm")
    y = lax.axis_index("space")
    x, z, core = tm // 8, lax.rem(tm // 2, 4), lax.rem(tm, 2)
    partner = tm + 1 - 2 * core

    def neighbour(axis, way):
        if axis == "x":
            return {"tm": turn(tm, 8 if way > 0 else 24, 32)}
        if axis == "z":
            return {"tm": x * 8 + turn(z, 1 if way > 0 else 3, 4) * 2 + core}
        return {"space": turn(y, 1 if way > 0 else 3, 4)}

    barrier = pltpu.get_barrier_semaphore()

    def greet(step, carry):
        pl.semaphore_signal(barrier, inc=1, device_id={"tm": turn(tm, step, 32)}, device_id_type=MESH)
        return carry

    lax.fori_loop(1, 32, greet, 0)
    for way in (1, -1):
        pl.semaphore_signal(barrier, inc=1, device_id=neighbour("y", way), device_id_type=MESH)

    def obs_copies(part, slot):
        rows = slice(START[part], START[part] + UNIT[part])
        pieces = []
        for other in range(4):
            at = (turn(x, slot, 4), turn(z, other, 4)) if part == 0 else (turn(x, other, 4), turn(z, slot, 4))
            pieces.append((at, rows, held[part].at[slot, other]))
        return pieces

    tasks = [(0, 2), (2, 2), (1, 2), (1, 1), (1, 3), (1, 0), (0, 1), (0, 3), (0, 0), (2, 1), (2, 3), (2, 0)]
    for yr in (2, 1, 3, 0):
        columns = pl.ds(pl.multiple_of(turn(y, yr, 4) * 256, 256), 256)
        for side, who in ((0, tm), (1, partner)):
            pltpu.make_async_copy(
                basis.at[who, :, columns], bas.at[yr, pl.ds(side * 512, 512)], bas_sem.at[yr]
            ).start()
    for part, slot in tasks:
        for (xi, zi), rows, to in obs_copies(part, slot):
            pltpu.make_async_copy(obs.at[xi, zi, core, rows], to.at[:, 0:512], own_sem.at[part, slot]).start()

    first = tm == 0
    for h in range(2):
        dec[h, 0:256, :] = decay[:, lane(h)]
        e1[3:4, lane(h)] = dec[h, 0:1, :]
        qv[h] = jnp.broadcast_to(q_ref[:, lane(h)], (256, 128))
        qv[h, 0:1, :] = jnp.where(first, pv_ref[:, lane(h)], q_ref[:, lane(h)])
        dec[h, 0:1, :] = jnp.where(first, 0.0, dec[h, 0:1, :])
    row = lax.broadcasted_iota(jnp.int32, (256, 256), 0)
    column = lax.broadcasted_iota(jnp.int32, (256, 256), 1)
    spread_mask = jnp.where(row == column, jnp.broadcast_to(mask[...].astype(F32), (256, 256)), 0.0).astype(BF16)
    flag[...] = jnp.dot(spread_mask, jnp.ones((256, 128), BF16), preferred_element_type=F32)

    def wide(ref, h):
        return jnp.broadcast_to(ref[:, lane(h)], (8, 128))

    blocks = [(g, h) for g in range(2) for h in range(2)]

    def steps(s, g):
        return pl.ds(g * 128 + s, 8, stride=16)

    def join(early, late):
        lead_e, spread_e, weight_e = early
        lead_l, spread_l, weight_l = late
        factor = 1.0 / (1.0 + spread_e * weight_l)
        return (
            lead_l * factor * lead_e,
            lead_l * lead_l * factor * spread_e + spread_l,
            lead_e * lead_e * factor * weight_l + weight_e,
        )

    def compose(s, carry):
        out = []
        for (g, h), early in zip(blocks, carry):
            seen, d, q = flag[steps(s, g), :], dec[h, steps(s, g), :], qv[h, steps(s, g), :]
            noise = wide(r_ref, h)
            den = 1.0 / (q + noise)
            retain = (noise + (1.0 - seen) * q) * den
            out.append(join(early, (retain * d, retain * q, seen * d * d * den)))
        return tuple(out)

    one, nil = jnp.ones((8, 128), F32), jnp.zeros((8, 128), F32)
    unit, zero = jnp.ones((1, 128), F32), jnp.zeros((1, 128), F32)
    chunks = lax.fori_loop(0, 16, compose, ((one, nil, nil),) * 4, unroll=2)
    totals = []
    for (g, h), parts in zip(blocks, chunks):
        for i in range(3):
            small[i, h, g * 8 : g * 8 + 8, :] = parts[i]
        totals.append(tuple(part[0:1] for part in parts))
    for k in range(1, 8):
        totals = [join(t, tuple(p[k : k + 1] for p in parts)) for t, parts in zip(totals, chunks)]
    for h in range(2):
        for i, value in enumerate(join(totals[h], totals[2 + h])):
            e1[i : i + 1, lane(h)] = value
        for i in range(3):
            small[11 + i, h, 0:1, :] = totals[h][i]

    pl.semaphore_wait(barrier, 33)

    def exchange(*pieces):
        for part, slot in pieces:
            for (xi, zi), rows, to in obs_copies(part, slot):
                pltpu.make_async_remote_copy(
                    obs.at[xi, zi, 1 - core, rows],
                    to.at[:, 512:1024],
                    psend_sem.at[part, slot],
                    part_sem.at[part, slot],
                    device_id={"tm": partner},
                    device_id_type=MESH,
                ).start()

    exchange(*tasks)

    def scatter(number, mine, gathered):
        gathered[tm] = mine[...]

        def push(step, carry):
            pltpu.make_async_remote_copy(
                mine,
                gathered.at[tm],
                esend_sem.at[number],
                erecv_sem.at[number],
                device_id={"tm": turn(tm, step, 32)},
                device_id_type=MESH,
            ).start()
            return carry

        lax.fori_loop(1, 32, push, 0)

    def gathered_wait(number, gathered, sem):
        some = gathered.at[pl.ds(0, 31)]
        pltpu.make_async_copy(some, some, sem.at[number]).wait()

    scatter(0, e1, g1)

    def obs_wait(part, slot):
        to = held[part].at[slot, :, :, pl.ds(0, 512)]
        pltpu.make_async_copy(to, to, own_sem.at[part, slot]).wait()
        pltpu.make_async_copy(to, to, part_sem.at[part, slot]).wait()

    def product(part, slot, j):
        u = UNIT[part]
        obs_slot, mode_slot = (j, slot) if part == 1 else (slot, j if part == 0 else lax.rem(4 - j, 4))
        return jnp.dot(held[part][obs_slot].reshape(4 * u, 1024), bas[mode_slot], preferred_element_type=F32)

    def place(part, stage, message, j):
        slot, half, _ = MESSAGES[message]
        u = UNIT[part]
        if stage == 2:
            return LAST[message] * u, u
        if stage == 0:
            return (slot * 4 + j) * (4 * u) + half * (2 * u), 2 * u
        return slot * 4 * u + half * 2 * u, 2 * u

    def number_of(part, stage, message, j):
        return part * 36 + (j * 6 if stage == 0 else 18 + 6 * stage) + message

    def index_of(stage, message, j):
        return j * 6 + message if stage == 0 else message

    def peak(block):
        return jnp.max(jnp.abs(block).reshape(-1, 8, 256), axis=0)

    def steps_of(top):
        top = jnp.maximum(jnp.max(top, axis=0, keepdims=True), TINY)
        return top * (1.0 / LIMIT), LIMIT / top

    def copies(part, stage, message, j):
        begin, rows = place(part, stage, message, j)
        if stage == 2:
            slot = LAST[message]
            to = {"tm": turn(tm, 8 * slot, 32) if ORDER[part][2] == "x" else x * 8 + turn(z, slot, 4) * 2 + core}
        else:
            way = MESSAGES[message][2]
            to = neighbour(ORDER[part][stage], -way if (part, stage) == (2, 1) else way)
        number = number_of(part, stage, message, j)
        return (
            pltpu.make_async_remote_copy(
                quant[part].at[pl.ds(pl.multiple_of(begin, 16), rows)],
                landed[part][stage].at[index_of(stage, message, j)],
                send_sem.at[part, stage],
                recv_sem.at[number],
                device_id=to,
                device_id_type=MESH,
            ),
            pltpu.make_async_remote_copy(
                scale_out.at[number],
                scale_in.at[number],
                ssend_sem.at[part, stage],
                srecv_sem.at[number],
                device_id=to,
                device_id_type=MESH,
            ),
        )

    def recv_wait(part, stage, message, j):
        for copy in copies(part, stage, message, j):
            copy.wait_recv()

    def send(part, stage, message, j=0, relayed=None):
        begin, rows = place(part, stage, message, j)
        number = number_of(part, stage, message, j)
        size = rows if stage == 2 else 64
        if relayed is not None:
            recv_wait(part, stage, relayed, j)
            factor = scale_in[number_of(part, stage, relayed, j)]

        def measure(k, top):
            at = pl.ds(pl.multiple_of(begin + k * size, 16), size)
            block = acc[part][at, :]
            if relayed is not None:
                came = landed[part][stage][index_of(stage, relayed, j), pl.ds(pl.multiple_of(k * size, 16), size), :]
                block = block + came.astype(F32) * factor
                acc[part][at, :] = block
            return jnp.maximum(top, peak(block))

        top = lax.fori_loop(0, rows // size, measure, jnp.zeros((8, 256), F32))
        scale_out[number], inverse = steps_of(top)

        def encode(k, carry):
            at = pl.ds(pl.multiple_of(begin + k * size, 16), size)
            quant[part][at, :] = jnp.round(acc[part][at, :] * inverse).astype(I16)
            return carry

        lax.fori_loop(0, rows // size, encode, 0)
        for copy in copies(part, stage, message, j):
            copy.start()

    def far(part, j):
        total = product(part, 2, j)
        u = UNIT[part]
        for message in (0, 1):
            begin, rows = place(part, 0, message, j)
            block = total[message * 2 * u : message * 2 * u + 2 * u]
            scale_out[number_of(part, 0, message, j)], inverse = steps_of(peak(block))
            at = pl.ds(pl.multiple_of(begin, 16), rows)
            quant[part][at, :] = jnp.round(block * inverse).astype(I16)
            for copy in copies(part, 0, message, j):
                copy.start()

    def rest(part, j):
        u = UNIT[part]

        def block(k, carry):
            slot = lax.rem(1 + 2 * k + 3 * (k // 2), 4)
            acc[part][pl.ds(pl.multiple_of((slot * 4 + j) * (4 * u), 16), 4 * u), :] = product(part, slot, j)
            return carry

        lax.fori_loop(0, 3, block, 0)
        send(part, 0, 3, j)
        send(part, 0, 4, j)

    def finish(part, stages, j=0):
        u = UNIT[part]
        rows, size = (u, u) if stages == (2,) else (2 * u, 64)
        for half, pair in enumerate(((0, 1, 2),) if stages == (2,) else ((2, 4), (3, 5))):
            begin = half * rows + (j * (4 * u) if stages == (0,) else 0)
            came = [(stage, message) for stage in stages for message in pair]
            for stage, message in came:
                recv_wait(part, stage, message, j)
            scales = [scale_in[number_of(part, stage, m, j)] for stage, m in came]

            def add(k, carry):
                at = pl.ds(pl.multiple_of(begin + k * size, 16), size)
                block = acc[part][at, :]
                for (stage, m), factor in zip(came, scales):
                    rows_in = pl.ds(pl.multiple_of(k * size, 16), size)
                    block = block + landed[part][stage][index_of(stage, m, j), rows_in, :].astype(F32) * factor
                acc[part][at, :] = block
                return carry

            lax.fori_loop(0, rows // size, add, 0)

    def variances():
        gathered_wait(0, g1, erecv_sem)

        def enter(k, v):
            lead, spread, weight = (g1[k, i : i + 1, :] for i in range(3))
            return jnp.where(k < tm, lead * lead * v / (1.0 + weight * v) + spread, v)

        v = lax.fori_loop(0, 31, enter, jnp.zeros((1, 256), F32), unroll=2)
        after = turn(tm, 1, 32)
        now = []
        for h in range(2):
            dec[h, 256:257, :] = jnp.where(tm == 31, 0.0, g1[after, 3:4, lane(h)])
            now.append(v[:, lane(h)])
        for h in range(2):
            lead, spread, weight = (small[11 + i, h, 0:1, :] for i in range(3))
            now.append(lead * lead * now[h] / (1.0 + weight * now[h]) + spread)
        for k in range(8):
            for b, (g, h) in enumerate(blocks):
                at = slice(g * 8 + k, g * 8 + k + 1)
                small[3, h, at, :] = now[b]
                if k < 7:
                    lead, spread, weight = (small[i, h, at, :] for i in range(3))
                    now[b] = lead * lead * now[b] / (1.0 + weight * now[b]) + spread

        def forward(s, carry):
            out = []
            for (g, h), (v, prefix) in zip(blocks, carry):
                seen, d, q = flag[steps(s, g), :], dec[h, steps(s, g), :], qv[h, steps(s, g), :]
                noise = wide(r_ref, h)
                vp = d * d * v + q
                den = 1.0 / (vp + noise)
                retain = (noise + (1.0 - seen) * vp) * den
                v = retain * vp
                a = retain * d
                prefix = prefix * a
                vv[h, steps(s, g), :] = v
                aa[h, steps(s, g), :] = a
                kk[h, steps(s, g), :] = seen * vp * den
                ap[h, steps(s, g), :] = prefix
                out.append((v, prefix))
            return tuple(out)

        starts = tuple((small[3, h, g * 8 : g * 8 + 8, :], one) for g, h in blocks)
        ends = lax.fori_loop(0, 16, forward, starts, unroll=2)
        for (g, h), (_, prefix) in zip(blocks, ends):
            small[4, h, g * 8 : g * 8 + 8, :] = prefix

    def smoother():
        def backward(i, carry):
            s = 15 - i
            out = []
            for (g, h), (var, pull, suffix) in zip(blocks, carry):
                nd, v = dec[h, steps(s + 1, g), :], vv[h, steps(s, g), :]
                process = wide(q_ref, h)
                inverse = 1.0 / (nd * nd * v + process)
                gain, w = v * nd * inverse, process * inverse
                var = gain * gain * var + v * w
                pull = gain * pull + w * ap[h, steps(s, g), :]
                suffix = gain * suffix
                gg[h, steps(s, g), :] = gain
                ww[h, steps(s, g), :] = w
                sv[h, steps(s, g), :] = var
                sm[h, steps(s, g), :] = pull
                gs[h, steps(s, g), :] = suffix
                out.append((var, pull, suffix))
            return tuple(out)

        heads = lax.fori_loop(0, 16, backward, ((nil, nil, one),) * 4, unroll=2)
        for (g, h), (var, pull, suffix) in zip(blocks, heads):
            rows = slice(g * 8, g * 8 + 8)
            small[5, h, rows, :], small[6, h, rows, :], small[7, h, rows, :] = pull, suffix, var
        for h in range(2):
            m = unit
            for k in range(16):
                small[8, h, k : k + 1, :] = m
                m = m * small[4, h, k : k + 1, :]
            e2[0:1, lane(h)] = m
            s_var, s_pull, s_suffix = zero, zero, unit
            for k in range(15, -1, -1):
                at = slice(k, k + 1)
                small[9, h, at, :], small[10, h, at, :] = s_pull, s_suffix
                g = small[6, h, at, :]
                s_var = small[7, h, at, :] + g * g * s_var
                s_pull = small[5, h, at, :] * small[8, h, at, :] + g * s_pull
                s_suffix = g * s_suffix
            e2[1:2, lane(h)], e2[2:3, lane(h)], e2[3:4, lane(h)] = s_pull, s_suffix, s_var
        scatter(1, e2, g2)

    def weights():
        gathered_wait(1, g2, erecv_sem)

        def down(i, carry):
            k = 31 - i
            var, w = carry
            prefix, suffix, spread = g2[k, 0:1, :], g2[k, 2:3, :], g2[k, 3:4, :]
            wm[k] = jnp.where(k < tm, w, 0.0)
            return (
                jnp.where(k > tm, spread + suffix * suffix * var, var),
                jnp.where(k < tm, prefix * w, w),
            )

        var, _ = lax.fori_loop(0, 32, down, (jnp.zeros((1, 256), F32), jnp.ones((1, 256), F32)), unroll=2)

        def up(k, w):
            ws[k] = jnp.where(k > tm, w, 0.0)
            return jnp.where(k > tm, g2[k, 2:3, :] * w, w)

        lax.fori_loop(0, 32, up, jnp.ones((1, 256), F32), unroll=2)

        def across(i, pull):
            k = 31 - i
            wl[k] = pull
            return ws[k] * g2[k, 1:2, :] + g2[k, 0:1, :] * pull

        lax.fori_loop(0, 32, across, jnp.zeros((1, 256), F32), unroll=2)
        for h in range(2):
            now = var[:, lane(h)]
            for k in range(15, -1, -1):
                rows, at = slice(k * 16, k * 16 + 16), slice(k, k + 1)
                g = gs[h, rows, :]
                prefix, pull, suffix = (small[i, h, at, :] for i in (8, 9, 10))
                made[6, rows, lane(h)] = jnp.log(sv[h, rows, :] + g * g * now)
                made[2, rows, lane(h)] = ap[h, rows, :] * prefix
                made[4, rows, lane(h)] = sm[h, rows, :] * prefix + g * pull
                made[5, rows, lane(h)] = g * suffix
                g = small[6, h, at, :]
                now = small[7, h, at, :] + g * g * now
        for i in (2, 4, 5, 6):
            put(i).start()

    def functionals():
        def gains_before(s, carry):
            out = []
            for (g, h), gamma in zip(blocks, carry):
                s0[h, steps(s, g), :] = gamma * ww[h, steps(s, g), :]
                out.append(gamma * gg[h, steps(s, g), :])
            return tuple(out)

        lax.fori_loop(0, 16, gains_before, (one,) * 4, unroll=2)

        def effects(i, carry):
            s = 15 - i
            out = []
            for (g, h), (after, effect) in zip(blocks, carry):
                a = aa[h, steps(s, g), :]
                effect = s0[h, steps(s, g), :] + effect
                al[h, steps(s, g), :] = after
                be[h, steps(s, g), :] = effect
                out.append((after * a, effect * a))
            return tuple(out)

        lax.fori_loop(0, 16, effects, ((one, nil),) * 4, unroll=2)
        for h in range(2):
            gamma, gammas = unit, []
            for k in range(16):
                gammas.append(gamma)
                gamma = gamma * small[6, h, k : k + 1, :]
            onward, pull = unit, zero
            for k in range(15, -1, -1):
                rows, at = slice(k * 16, k * 16 + 16), slice(k, k + 1)
                after = al[h, rows, :]
                left, right = after * onward, gammas[k] * be[h, rows, :] + after * pull
                if k == 0:
                    small[14, h, 0:1, :], small[15, h, 0:1, :] = left[0:1], right[0:1]
                al[h, rows, :] = left * kk[h, rows, :]
                be[h, rows, :] = right * kk[h, rows, :]
                pull = gammas[k] * small[5, h, at, :] + small[4, h, at, :] * pull
                onward = onward * small[4, h, at, :]

    for yr in range(4):
        pltpu.make_async_copy(bas.at[yr], bas.at[yr], bas_sem.at[yr]).wait()

    obs_wait(0, 2)
    obs_wait(2, 2)

    def farthest(i, carry):
        j = sub_block(i)
        far(0, j)
        far(2, j)
        obs_wait(1, j)
        far(1, j)
        return carry

    lax.fori_loop(0, 4, farthest, 0)
    for part in (0, 2):
        for slot in (1, 3, 0):
            obs_wait(part, slot)

    def round_of(i, carry):
        @pl.when(i < 4)
        def _():
            j = sub_block(i)
            for part in TURNS:
                rest(part, j)
            for part in TURNS:
                send(part, 0, 2, j, relayed=0)
                send(part, 0, 5, j, relayed=1)

        pl.when(i == 0)(variances)
        pl.when(i == 1)(smoother)

        @pl.when((i >= 1) & (i < 4))
        def _():
            j = sub_block(i - 1)
            for part in TURNS:
                finish(part, (0,), j)

                @pl.when(i == 1)
                def _():
                    send(part, 1, 0)
                    send(part, 1, 1)

                @pl.when(i == 2)
                def _():
                    send(part, 1, 3)
                    send(part, 1, 2, relayed=0)

                @pl.when(i == 3)
                def _():
                    send(part, 1, 4)
                    send(part, 1, 5, relayed=1)

        return carry

    lax.fori_loop(0, 4, round_of, 0)
    weights()
    functionals()

    for part in TURNS:
        finish(part, (0, 1))
        for message in range(3):
            send(part, 2, message)
    ends, heads = [nil, nil], [nil, nil]
    for part in TURNS:
        finish(part, (2,))
        rows = slice(START[part], START[part] + UNIT[part])
        block = acc[part][0 : UNIT[part], :]
        made[0, rows, :] = block
        for h in range(2):
            half = block[:, lane(h)]
            cc[h, rows, :] = half * kk[h, rows, :]
            ends[h] = ends[h] + jnp.sum((half * al[h, rows, :]).reshape(-1, 8, 128), axis=0)
            heads[h] = heads[h] + jnp.sum((half * be[h, rows, :]).reshape(-1, 8, 128), axis=0)

    for h in range(2):
        pv, r = pv_ref[:, lane(h)], r_ref[:, lane(h)]
        retain = (r + (1.0 - flag[0:1, :]) * pv) / (pv + r)
        prior = jnp.where(first, retain * pm_ref[:, lane(h)], 0.0)
        cc[h, 0:1, :] = cc[h, 0:1, :] + prior
        e3[0:1, lane(h)] = jnp.sum(ends[h], axis=0, keepdims=True) + small[14, h, 0:1, :] * prior
        e3[1:2, lane(h)] = jnp.sum(heads[h], axis=0, keepdims=True) + small[15, h, 0:1, :] * prior
    scatter(2, e3, g3)
    put(0).start()

    def mean_forward(s, carry):
        out = []
        for (g, h), m in zip(blocks, carry):
            m = aa[h, steps(s, g), :] * m + cc[h, steps(s, g), :]
            ll[h, steps(s, g), :] = m
            out.append(m)
        return tuple(out)

    tails = lax.fori_loop(0, 16, mean_forward, (nil,) * 4, unroll=4)

    def mean_backward(i, carry):
        s = 15 - i
        out = []
        for (g, h), m in zip(blocks, carry):
            m = gg[h, steps(s, g), :] * m + ww[h, steps(s, g), :] * ll[h, steps(s, g), :]
            s0[h, steps(s, g), :] = m
            out.append(m)
        return tuple(out)

    fronts = lax.fori_loop(0, 16, mean_backward, (nil,) * 4, unroll=4)
    into, back = ([None] * 16, [None] * 16), ([None] * 16, [None] * 16)
    for h in range(2):
        m, s = zero, zero
        for k in range(16):
            into[h][k] = m
            m = small[4, h, k : k + 1, :] * m + tails[k // 8 * 2 + h][k % 8 : k % 8 + 1]
        for k in range(15, -1, -1):
            back[h][k] = s
            front = fronts[k // 8 * 2 + h][k % 8 : k % 8 + 1]
            s = front + small[5, h, k : k + 1, :] * into[h][k] + small[6, h, k : k + 1, :] * s
    for h in range(2):
        for k in range(16):
            rows = slice(k * 16, k * 16 + 16)
            made[1, rows, lane(h)] = ll[h, rows, :] + ap[h, rows, :] * into[h][k]
            made[3, rows, lane(h)] = s0[h, rows, :] + sm[h, rows, :] * into[h][k] + gs[h, rows, :] * back[h][k]
    put(1).start()
    put(3).start()
    for part in range(3):
        u = UNIT[part]
        for stage, (begin, rows, base, count) in enumerate(
            ((16 * u, 48 * u, 0, 24), (4 * u, 12 * u, 24, 6), (u, 3 * u, 30, 3))
        ):
            some = quant[part].at[pl.ds(begin, rows)]
            pltpu.make_async_copy(some, some, send_sem.at[part, stage]).wait()
            some = scale_out.at[pl.ds(part * 36 + base, count)]
            pltpu.make_async_copy(some, some, ssend_sem.at[part, stage]).wait()
    for part, slot in tasks:
        to = held[part].at[slot, :, :, pl.ds(0, 512)]
        pltpu.make_async_copy(to, to, psend_sem.at[part, slot]).wait()
    gathered_wait(0, g1, esend_sem)
    gathered_wait(1, g2, esend_sem)
    gathered_wait(2, g3, esend_sem)
    gathered_wait(2, g3, erecv_sem)
    m_in, s_in = [jnp.zeros((1, 256), F32)] * 4, [jnp.zeros((1, 256), F32)] * 4
    for k in range(32):
        left, right = g3[k, 0:1, :], g3[k, 1:2, :]
        m_in[k % 4] = m_in[k % 4] + wm[k] * left
        s_in[k % 4] = s_in[k % 4] + (ws[k] * right + wl[k] * left)
    last[0:1, :] = (m_in[0] + m_in[1]) + (m_in[2] + m_in[3])
    last[1:2, :] = (s_in[0] + s_in[1]) + (s_in[2] + s_in[3])
    put(7).start()
    for i in range(8):
        put(i).wait()


def apply_starts(*refs):
    ins, outs, (got, start, into, back, in_sem, out_sem) = refs[:8], refs[8:12], refs[12:]

    def take(i):
        return pltpu.make_async_copy(ins[i], start if i == 7 else got.at[i], in_sem.at[i])

    def give(i):
        source = (got.at[0], into, back, got.at[6])[i]
        return pltpu.make_async_copy(source, outs[i], out_sem.at[i])

    order = (7, 1, 2, 3, 4, 5, 0, 6)
    for i in order:
        take(i).start()
    for i in (7, 1, 2):
        take(i).wait()
    m_in, s_in = start[0:1, :], start[1:2, :]
    into[...] = got[1] + got[2] * m_in
    give(1).start()
    for i in (3, 4, 5):
        take(i).wait()
    back[...] = got[3] + got[4] * m_in + got[5] * s_in
    give(2).start()
    take(0).wait()
    give(0).start()
    take(6).wait()
    give(3).start()
    for i in range(4):
        give(i).wait()


def body(observations, pod_basis, decay, step_mask, process_var, obs_var, prior_mean, prior_var):
    block = jax.ShapeDtypeStruct((256, 256), F32)
    vmem = pl.BlockSpec(memory_space=pltpu.VMEM)
    anywhere = pl.BlockSpec(memory_space=pl.ANY)
    plane = pltpu.VMEM((2, 256, 128), F32)
    landing = [
        pltpu.VMEM(shape, I16) for u in UNIT for shape in ((24, 2 * u, 256), (6, 2 * u, 256), (3, u, 256))
    ]
    dma = pltpu.SemaphoreType.DMA
    scratch = [
        pltpu.VMEM((7, 256, 256), F32),
        pltpu.VMEM((2, 256), F32),
        dma((8,)),
        *[pltpu.VMEM((rows, 256), F32) for rows in ROWS],
        *[pltpu.VMEM((rows, 256), I16) for rows in ROWS],
        *landing,
        *[pltpu.VMEM((4, 4, u, 1024), BF16) for u in UNIT],
        pltpu.VMEM((4, 1024, 256), BF16),
        pltpu.VMEM((108, 1, 256), F32),
        pltpu.VMEM((108, 1, 256), F32),
        pltpu.VMEM((2, 288, 128), F32),
        pltpu.VMEM((256, 128), F32),
        *[plane] * 15,
        pltpu.VMEM((16, 2, 16, 128), F32),
        pltpu.VMEM((4, 256), F32),
        pltpu.VMEM((4, 256), F32),
        pltpu.VMEM((2, 256), F32),
        pltpu.VMEM((32, 4, 256), F32),
        pltpu.VMEM((32, 4, 256), F32),
        pltpu.VMEM((32, 2, 256), F32),
        *[pltpu.VMEM((32, 1, 256), F32)] * 3,
        dma((3, 4)),
        dma((3, 4)),
        dma((3, 4)),
        dma((4,)),
        dma((3, 3)),
        dma((108,)),
        dma((3, 3)),
        dma((108,)),
        dma((3,)),
        dma((3,)),
    ]
    made = pl.pallas_call(
        kernel,
        out_shape=[block] * 7 + [jax.ShapeDtypeStruct((2, 256), F32)],
        in_specs=[anywhere, anywhere, *[vmem] * 6],
        out_specs=[anywhere] * 8,
        scratch_shapes=scratch,
        compiler_params=pltpu.CompilerParams(
            collective_id=0, has_side_effects=True, vmem_limit_bytes=60 * 2**20
        ),
    )(
        observations.reshape(4, 4, 2, 256, 512),
        pod_basis.reshape(32, 512, 1024),
        decay,
        step_mask.reshape(1, 256),
        process_var.reshape(1, 256),
        obs_var.reshape(1, 256),
        prior_mean.reshape(1, 256),
        prior_var.reshape(1, 256),
    )
    return tuple(
        pl.pallas_call(
            apply_starts,
            out_shape=[block] * 4,
            in_specs=[anywhere] * 8,
            out_specs=[anywhere] * 4,
            scratch_shapes=[
                pltpu.VMEM((7, 256, 256), F32),
                pltpu.VMEM((2, 256), F32),
                pltpu.VMEM((256, 256), F32),
                pltpu.VMEM((256, 256), F32),
                dma((8,)),
                dma((4,)),
            ],
            compiler_params=pltpu.CompilerParams(vmem_limit_bytes=60 * 2**20),
        )(*made)
    )


def solution(mesh):
    return jax.shard_map(
        body,
        mesh=mesh,
        in_specs=(
            P(None, "tm", "space", None),
            P(None, "space", None, None),
            P("tm", "space"),
            P("tm"),
            P("space"),
            P("space"),
            P("space"),
            P("space"),
        ),
        out_specs=(P("tm", "space"), P("tm", "space"), P("tm", "space"), P("tm", "space")),
        check_vma=False,
    )
```
